32 devices in a mesh: pix: 4 (over z), mode: 8 (over y, x, core).
Axes of the slice: x: 2, y: 2, z: 4, core: 2. Of those that a mesh axis runs over, the one named last changes fastest.
Arguments:
- frames: float32 [4, 4096, 8192], P(None, 'pix', 'mode'), may hold values from 0 to 500, as said below
- phase_steps: int32 [4], replicated, may hold values from 0 to 3, each once
- pattern_rows: int32 [8192], replicated, may hold values from 0 to 8191, each once
- probes: float32 [2, 32, 8192], replicated, may hold values from -6 to 6
Outputs:
- channels: float32 [2, 32, 8192], replicated
- fields: float32 [2, 32, 4096], P(None, None, ('pix', 'mode'))
- strengths: float32 [32], replicated
The draws below stay inside these ranges and needn't reach their ends.
Inputs may be any that keep to these rules, and one draw needn't show every extreme that they name: `phase_steps`: each frame has its own phase step. `pattern_rows`: every Hadamard row is displayed exactly once. `frames`: intensities are not negative.
All inputs are finite; a program needn't handle non-finite values.
Results may differ from the reference program's by a relative error of at most 0.0003.
Values sent between devices are 32-bit elements; how exact they have to be, the bound alone decides.
No kernel may reach another device: no remote copies, remote signals or barrier semaphores. Data moves between devices by JAX's collectives and lax.ppermute only.
A program may use at most 128 MiB of HBM per device.

```python
import math
import jax
import jax.numpy as jnp
from jax import lax

M = 8192
HB = 128
STEPS = 4
K = 32
ITERS = 2
P_SIZE = 4096


def draw_frames(key, part):
    row_key, col_key, light_key = jax.random.split(key, 3)
    position = jnp.arange(P_SIZE, dtype=jnp.float32) / P_SIZE
    growth = jnp.exp(math.log(3.0) * position)
    row_scale = jnp.exp(jax.random.uniform(row_key, (P_SIZE,), jnp.float32, math.log(0.3), math.log(3.0))) * growth
    col_scale = jnp.exp(jax.random.uniform(col_key, (M,), jnp.float32, math.log(0.3), math.log(3.0)))
    intensity = jax.random.uniform(light_key, (STEPS, P_SIZE, M), jnp.float32, 0.0, 2.0)
    return (intensity * row_scale[None, :, None] * col_scale[None, None, :]).astype(jnp.float32)


def bell_draw(key, shape, scale, reach, kind=jnp.bfloat16):
    result = scale * jax.random.normal(key, shape, jnp.float32)
    return jnp.clip(result, min=-reach, max=reach).astype(kind)


def setup_inputs(seed: int = 0) -> dict:
    keys = jax.random.split(jax.random.key(seed), 5)
    return {
        "frames": draw_frames(jax.random.fold_in(keys[4], 71), 0),
        "phase_steps": jax.random.permutation(keys[1], STEPS).astype(jnp.int32),
        "pattern_rows": jax.random.permutation(keys[2], M).astype(jnp.int32),
        "probes": bell_draw(keys[3], (2, K, M), 1.0, 6.0, jnp.float32),
    }


precise = lax.Precision.HIGHEST

def demodulate(frames, phase_steps):
    cosine = (phase_steps == 0).astype(jnp.float32) - (phase_steps == 2).astype(jnp.float32)
    sine_part = (phase_steps == 1).astype(jnp.float32) - (phase_steps == 3).astype(jnp.float32)
    real_part = cosine[0] * frames[0]
    imag_part = sine_part[0] * frames[0]
    for frame_index in range(1, frames.shape[0]):
        real_part = real_part + cosine[frame_index] * frames[frame_index]
        imag_part = imag_part + sine_part[frame_index] * frames[frame_index]
    return (0.25 * real_part, 0.25 * imag_part)

def sign_table(table_order):
    positions = jnp.arange(table_order, dtype=jnp.int32)
    common = positions[:, None] & positions[None, :]
    parity = jnp.zeros((table_order, table_order), jnp.int32)
    for bit_place in range(table_order.bit_length() - 1):
        parity = parity + (common >> bit_place & 1)
    return (1 - 2 * (parity & 1)).astype(jnp.float32)

def hadamard_rows(values):
    length = values.shape[-1]
    leading = values.shape[:-1]
    inner_signs = sign_table(HB)
    outer_signs = sign_table(length // HB)
    shaped = values.reshape((-1, length // HB, HB))
    shaped = jnp.matmul(shaped, inner_signs, precision=precise)
    shaped = jnp.einsum('ab,nbc->nac', outer_signs, shaped, precision=precise)
    return shaped.reshape(leading + (length,)) * (1.0 / math.sqrt(length))

def contract_last(first_arg, second_arg):
    return lax.dot_general(first_arg, second_arg, (((1,), (1,)), ((), ())), precision=precise)

def forward(matrix, vectors):
    real_out = contract_last(vectors[0], matrix[0]) - contract_last(vectors[1], matrix[1])
    imag_out = contract_last(vectors[1], matrix[0]) + contract_last(vectors[0], matrix[1])
    return jnp.stack([real_out, imag_out])

def backward(matrix, images):
    real_out = jnp.dot(images[0], matrix[0], precision=precise) + jnp.dot(images[1], matrix[1], precision=precise)
    imag_out = jnp.dot(images[1], matrix[0], precision=precise) - jnp.dot(images[0], matrix[1], precision=precise)
    return jnp.stack([real_out, imag_out])

def orthonormal(vectors):
    mode_count = vectors.shape[2]
    stacked = jnp.concatenate([vectors[0], vectors[1]], axis=1)
    gram_matrix = jnp.dot(stacked, stacked.T, precision=precise)
    factor = jnp.linalg.cholesky(gram_matrix)
    solved = lax.linalg.triangular_solve(factor, stacked, left_side=True, lower=True)
    return jnp.stack([solved[:, :mode_count], solved[:, mode_count:]])

def reference(frames, phase_steps, pattern_rows, probes):
    real_part, imag_part = demodulate(frames, phase_steps)
    positions = jnp.arange(M, dtype=jnp.int32)
    inverse = jnp.zeros((M,), jnp.int32).at[pattern_rows].set(positions)
    ordered = jnp.take(jnp.stack([real_part, imag_part]), inverse, axis=2)
    matrix = hadamard_rows(ordered)
    current = orthonormal(probes)
    for iteration in range(ITERS):
        images = forward(matrix, current)
        current = orthonormal(backward(matrix, images))
    fields = forward(matrix, current)
    strengths = lax.optimization_barrier(jnp.sum(fields * fields, axis=(0, 2))) / P_SIZE
    channels = math.sqrt(M) * current
    return (channels, fields, strengths)
```

```python
import functools
import math

import jax
import jax.numpy as jnp
from jax import lax
from jax.experimental import pallas as pl
from jax.experimental.pallas import tpu as pltpu
from jax.sharding import PartitionSpec as P

HB = 128
ITERS = 2
BLOCK = 256
F32 = jnp.float32
BF16 = jnp.bfloat16

precise = lax.Precision.HIGHEST
NT = (((1,), (1,)), ((), ()))
NN = (((1,), (0,)), ((), ()))
VMEM = pl.BlockSpec(memory_space=pltpu.VMEM)
SMEM = pl.BlockSpec(memory_space=pltpu.SMEM)


def dot(a, b, dims):
    return lax.dot_general(a, b, dims, preferred_element_type=F32)


def exact(a, b, dims):
    return lax.dot_general(a, b, dims, precision=precise, preferred_element_type=F32)


def split(values):
    high = values.astype(BF16)
    return high, (values - high.astype(F32)).astype(BF16)


def sign_table(order):
    row = lax.broadcasted_iota(jnp.int32, (order, order), 0)
    common = row & lax.broadcasted_iota(jnp.int32, (order, order), 1)
    parity = common
    shift = 16
    while shift:
        parity = parity ^ (parity >> shift)
        shift //= 2
    return (1 - 2 * (parity & 1)).astype(F32)


def butterfly(ref, count, size):
    step = 1
    while step < count:
        radix = 8 if step * 8 <= count else count // step
        groups = count // radix

        def body(g, carry, step=step, radix=radix):
            low = g % step
            base = (g // step) * (step * radix) + low
            for s in range(size // 8):
                at = [pl.multiple_of((base + r * step) * size + s * 8, 8) for r in range(radix)]
                v = [ref[pl.ds(a, 8), :] for a in at]
                half = 1
                while half < radix:
                    v = [
                        v[r] + v[r + half] if not r & half else v[r - half] - v[r]
                        for r in range(radix)
                    ]
                    half *= 2
                for a, x in zip(at, v):
                    ref[pl.ds(a, 8), :] = x
            return carry

        lax.fori_loop(0, groups, body, 0)
        step *= radix


def rows_of(vectors):
    return jnp.concatenate([vectors, jnp.zeros_like(vectors)], axis=0).T


def start_kernel(scale, idx_ref, probes_ref, u_ref, w_ref, g_ref):
    modes = probes_ref.shape[1]
    outer = modes // HB
    count = u_ref.shape[1]
    signs = sign_table(HB).astype(BF16)

    def inner(i, carry):
        at = pl.multiple_of(i * HB, HB)
        high, low = split(rows_of(probes_ref[:, pl.ds(at, HB)]))
        w_ref[pl.ds(at, HB), :] = dot(signs, high, NN) + dot(signs, low, NN)
        return carry

    lax.fori_loop(0, outer, inner, 0)
    butterfly(w_ref, outer, HB)

    def gather(t, carry):
        at = pl.multiple_of(t * 8, 8)
        for q in range(8):
            g_ref[pl.ds(at + q, 1), :] = w_ref[pl.ds(idx_ref[at + q], 1), :]
        return carry

    lax.fori_loop(0, count // 8, gather, 0)
    for b in range(count // HB):
        part = g_ref[b * HB : (b + 1) * HB, :].T
        u_ref[:, b * HB : (b + 1) * HB] = part[: u_ref.shape[0]] * scale


def start_vectors(idx, probes, scale):
    vectors, modes = probes.shape
    count = idx.shape[0]
    return pl.pallas_call(
        functools.partial(start_kernel, scale),
        out_shape=jax.ShapeDtypeStruct((vectors, count), F32),
        in_specs=[SMEM, VMEM],
        out_specs=VMEM,
        scratch_shapes=[pltpu.VMEM((modes, 128), F32), pltpu.VMEM((count, 128), F32)],
        compiler_params=pltpu.CompilerParams(vmem_limit_bytes=16 << 20),
    )(idx, probes)


def end_kernel(idx_ref, x_ref, inv_ref, out_ref, s_ref, w_ref):
    chunks, vectors, count = x_ref.shape
    modes = out_ref.shape[1]
    outer = modes // HB
    half = vectors // 2
    signs = sign_table(HB).astype(BF16)
    per = count // HB

    def turn(i, carry):
        c = i // per
        at = pl.multiple_of((i % per) * HB, HB)
        to = pl.multiple_of(i * HB, HB)
        s_ref[pl.ds(to, HB), :] = rows_of(x_ref[c, :, pl.ds(at, HB)])
        return carry

    lax.fori_loop(0, modes // HB, turn, 0)

    def scatter(t, carry):
        at = pl.multiple_of(t * 8, 8)
        for q in range(8):
            w_ref[pl.ds(idx_ref[at + q], 1), :] = s_ref[pl.ds(at + q, 1), :]
        return carry

    lax.fori_loop(0, modes // 8, scatter, 0)
    butterfly(w_ref, outer, HB)

    def inner(i, carry):
        at = pl.multiple_of(i * HB, HB)
        high, low = split(w_ref[pl.ds(at, HB), :].T[:vectors])
        both = dot(jnp.concatenate([high, low], axis=0), signs, NN)
        total = both[:vectors] + both[vectors:]
        out_ref[:half, pl.ds(at, HB)] = exact(inv_ref[...], total[:half], NN)
        out_ref[half:, pl.ds(at, HB)] = exact(inv_ref[...], total[half:], NN)
        return carry

    lax.fori_loop(0, outer, inner, 0)


def end_vectors(idx, gathered, inv):
    chunks, vectors, count = gathered.shape
    modes = chunks * count
    return pl.pallas_call(
        end_kernel,
        out_shape=jax.ShapeDtypeStruct((vectors, modes), F32),
        in_specs=[SMEM, VMEM, VMEM],
        out_specs=VMEM,
        scratch_shapes=[pltpu.VMEM((modes, 128), F32), pltpu.VMEM((modes, 128), F32)],
        compiler_params=pltpu.CompilerParams(vmem_limit_bytes=24 << 20),
    )(idx, gathered, inv)


def stack_forward(u):
    half = u.shape[0] // 2
    turned = jnp.concatenate([-u[half:], u[:half]], axis=0)
    uh, ul = split(u)
    th, tl = split(turned)
    return jnp.concatenate([uh, ul], axis=0), jnp.concatenate([th, tl], axis=0)


def apply_forward(both, turned, dh, dl):
    n = both.shape[0] // 2
    wide = dot(both, dh[0], NT) + dot(turned, dh[1], NT)
    low = dot(both[:n], dl[0], NT) + dot(turned[:n], dl[1], NT)
    return wide[:n] + wide[n:] + low


def demod_kernel(inv_ref, f0, f1, f2, f3, u_ref, dh_ref, dl_ref, img_ref, b_ref, t_ref):
    @pl.when(pl.program_id(0) == 0)
    def _():
        b_ref[...], t_ref[...] = stack_forward(u_ref[...])

    for part, plus, minus in ((0, f0, f2), (1, f1, f3)):
        high, low = split(0.25 * (plus[0] - minus[0]))
        dh_ref[part] = high
        dl_ref[part] = low
    img_ref[...] = apply_forward(b_ref[...], t_ref[...], dh_ref, dl_ref)


def demodulate(steps_at, frames, u):
    steps, rows, cols = frames.shape
    vectors = u.shape[0]
    block = min(BLOCK, rows)

    def frame(s):
        return pl.BlockSpec((1, block, cols), lambda i, at: (at[s], i, 0))

    planes = pl.BlockSpec((2, block, cols), lambda i, at: (0, i, 0))
    return pl.pallas_call(
        demod_kernel,
        grid_spec=pltpu.PrefetchScalarGridSpec(
            num_scalar_prefetch=1,
            grid=(rows // block,),
            in_specs=[frame(0), frame(1), frame(2), frame(3)]
            + [pl.BlockSpec((vectors, cols), lambda i, at: (0, 0))],
            out_specs=[planes, planes, pl.BlockSpec((vectors, block), lambda i, at: (0, i))],
            scratch_shapes=[pltpu.VMEM((2 * vectors, cols), BF16)] * 2,
        ),
        out_shape=[
            jax.ShapeDtypeStruct((2, rows, cols), BF16),
            jax.ShapeDtypeStruct((2, rows, cols), BF16),
            jax.ShapeDtypeStruct((vectors, rows), F32),
        ],
        compiler_params=pltpu.CompilerParams(vmem_limit_bytes=24 << 20),
    )(steps_at, frames, frames, frames, frames, u)


def forward_kernel(u_ref, dh_ref, dl_ref, img_ref, b_ref, t_ref):
    @pl.when(pl.program_id(0) == 0)
    def _():
        b_ref[...], t_ref[...] = stack_forward(u_ref[...])

    img_ref[...] = apply_forward(b_ref[...], t_ref[...], dh_ref, dl_ref)


def forward(u, dh, dl):
    _, rows, cols = dh.shape
    vectors = u.shape[0]
    block = min(BLOCK, rows)
    planes = pl.BlockSpec((2, block, cols), lambda i: (0, i, 0))
    return pl.pallas_call(
        forward_kernel,
        grid=(rows // block,),
        in_specs=[pl.BlockSpec((vectors, cols), lambda i: (0, 0)), planes, planes],
        out_specs=pl.BlockSpec((vectors, block), lambda i: (0, i)),
        scratch_shapes=[pltpu.VMEM((2 * vectors, cols), BF16)] * 2,
        out_shape=jax.ShapeDtypeStruct((vectors, rows), F32),
        compiler_params=pltpu.CompilerParams(vmem_limit_bytes=16 << 20),
    )(u, dh, dl)


def backward_kernel(inv_ref, img_ref, dh_ref, dl_ref, ret_ref):
    vectors = img_ref.shape[0]
    half = vectors // 2
    real = exact(inv_ref[...], img_ref[:half], NN)
    imag = exact(inv_ref[...], img_ref[half:], NN)
    total = None
    for part, rows in ((0, [real, imag]), (1, [imag, -real])):
        high, low = split(jnp.concatenate(rows, axis=0))
        wide = dot(jnp.concatenate([high, low], axis=0), dh_ref[part], NN)
        here = wide[:vectors] + wide[vectors:] + dot(high, dl_ref[part], NN)
        total = here if total is None else total + here

    @pl.when(pl.program_id(0) == 0)
    def _():
        ret_ref[...] = total

    @pl.when(pl.program_id(0) != 0)
    def _():
        ret_ref[...] += total


def backward(inv, images, dh, dl):
    _, rows, cols = dh.shape
    vectors = images.shape[0]
    block = min(BLOCK, rows)
    planes = pl.BlockSpec((2, block, cols), lambda i: (0, i, 0))
    return pl.pallas_call(
        backward_kernel,
        grid=(rows // block,),
        in_specs=[
            pl.BlockSpec(inv.shape, lambda i: (0, 0)),
            pl.BlockSpec((vectors, block), lambda i: (0, i)),
            planes,
            planes,
        ],
        out_specs=pl.BlockSpec((vectors, cols), lambda i: (0, 0)),
        out_shape=jax.ShapeDtypeStruct((vectors, cols), F32),
        compiler_params=pltpu.CompilerParams(vmem_limit_bytes=16 << 20),
    )(inv, images, dh, dl)


def gram(vectors):
    half = vectors.shape[0] // 2
    return exact(vectors[:half], vectors[:half], NT) + exact(vectors[half:], vectors[half:], NT)


def inverse_factor(gram_matrix):
    factor = jnp.linalg.cholesky(gram_matrix)
    eye = jnp.eye(gram_matrix.shape[0], dtype=F32)
    return lax.linalg.triangular_solve(factor, eye, left_side=True, lower=True)


def normalise(inv, vectors):
    half = inv.shape[0]
    return jnp.concatenate([exact(inv, vectors[:half], NN), exact(inv, vectors[half:], NN)], axis=0)


def flip(n, bit):
    return [(i, i ^ bit) for i in range(n)]


def pick(pieces, here, n):
    bit = 1
    while bit < n:
        odd = (here & bit) != 0
        pieces = [jnp.where(odd, pieces[b ^ bit], pieces[b]) for b in range(n)]
        bit *= 2
    return pieces


def scatter_sum(blocks, axis, step, n):
    size = lax.axis_size(axis)
    here = (lax.axis_index(axis) // step) % n
    mine = pick(blocks, here, n)
    total = mine[0]
    for b in range(1, n):
        total = total + lax.ppermute(mine[b], axis, flip(size, b * step))
    return total


def gather_all(block, axis, step, n):
    size = lax.axis_size(axis)
    here = (lax.axis_index(axis) // step) % n
    pieces = [block] + [lax.ppermute(block, axis, flip(size, b * step)) for b in range(1, n)]
    return pick(pieces, here, n)


def share_sum(block, axis, step, n):
    size = lax.axis_size(axis)
    total = block
    for b in range(1, n):
        total = total + lax.ppermute(block, axis, flip(size, b * step))
    return total


def double_sum(block, axis):
    size = lax.axis_size(axis)
    bit = 1
    while bit < size:
        block = block + lax.ppermute(block, axis, flip(size, bit))
        bit *= 2
    return block


def sum_pix(x):
    n = lax.axis_size("pix")
    if n != 4:
        return double_sum(x, "pix")
    rows = x.shape[0] // n
    mine = scatter_sum([x[i * rows : (i + 1) * rows] for i in range(n)], "pix", 1, n)
    return jnp.concatenate(gather_all(mine, "pix", 1, n), axis=0)


def pack(gram_matrix, width):
    return jnp.pad(gram_matrix.reshape(1, -1), ((0, 7), (0, width - gram_matrix.size)))


def sum_mode(x, extra=None):
    n = lax.axis_size("mode")
    rows, cols = x.shape
    if n != 8:
        total = double_sum(x, "mode")
        return total, (None if extra is None else double_sum(extra, "mode"))
    half = rows // 2
    odd = (lax.axis_index("mode") % 2) != 0
    mine = jnp.where(odd, x[half:], x[:half])
    other = jnp.where(odd, x[:half], x[half:])
    if extra is not None:
        k = extra.shape[0]
        row = pack(extra, cols)
        mine = jnp.concatenate([mine, row], axis=0)
        other = jnp.concatenate([other, row], axis=0)
    chip = mine + lax.ppermute(other, "mode", flip(n, 1))
    chip = share_sum(chip, "mode", 2, 4)
    mine = chip[:half]
    other = lax.ppermute(mine, "mode", flip(n, 1))
    total = jnp.concatenate([jnp.where(odd, other, mine), jnp.where(odd, mine, other)], axis=0)
    if extra is None:
        return total, None
    return total, chip[half, : k * k].reshape(k, k)


def local(frames, phase_steps, pattern_rows, probes):
    columns = frames.shape[2]
    rows = frames.shape[1]
    groups = lax.axis_size("mode")
    pixels = rows * lax.axis_size("pix")
    modes_total = columns * groups
    k = probes.shape[1]
    vectors = 2 * k
    probes = probes.reshape(vectors, modes_total)
    here = lax.axis_index("mode")
    steps_at = jnp.sum(
        jnp.where(phase_steps[None, :] == jnp.arange(4)[:, None], jnp.arange(4)[None, :], 0), axis=1
    ).astype(jnp.int32)
    my_rows = lax.dynamic_slice_in_dim(pattern_rows, here * columns, columns)
    u = start_vectors(my_rows, probes, 1.0 / math.sqrt(modes_total))
    dh, dl, images = demodulate(steps_at, frames, u)
    inv = inverse_factor(gram(probes))
    images, _ = sum_mode(images)
    returned = sum_pix(backward(inv, images, dh, dl))
    for iteration in range(1, ITERS):
        images = forward(returned, dh, dl)
        images, gram_matrix = sum_mode(images, gram(returned))
        inv = inverse_factor(gram_matrix)
        returned = sum_pix(backward(inv, images, dh, dl))
    images = forward(returned, dh, dl)
    images, gram_matrix = sum_mode(images, gram(returned))
    inv = inverse_factor(gram_matrix)
    width = rows // groups
    fields = normalise(inv, lax.dynamic_slice_in_dim(images, here * width, width, 1))
    power = jnp.sum(fields * fields, axis=1)
    power = jnp.broadcast_to((power[:k] + power[k:])[None, :], (8, k))
    power = double_sum(double_sum(power, "mode"), "pix")
    strengths = power[0] / pixels
    third = vectors // 8 * 3 // 8 * 8
    parts = [(0, third), (third, 2 * third), (2 * third, vectors)]
    gathered = jnp.concatenate(
        [lax.all_gather(returned[a:b], "mode", tiled=False) for a, b in parts], axis=1
    )
    channels = end_vectors(pattern_rows, gathered, inv)
    return (channels.reshape(2, k, modes_total), fields.reshape(2, k, width), strengths)


def solution(mesh):
    in_specs = (P(None, "pix", "mode"), P(), P(), P())
    out_specs = (P(), P(None, None, ("pix", "mode")), P())
    return jax.shard_map(local, mesh=mesh, in_specs=in_specs, out_specs=out_specs, check_vma=False)
```

```python
import functools
import math

import jax
import jax.numpy as jnp
from jax import lax
from jax.experimental import pallas as pl
from jax.experimental.pallas import tpu as pltpu
from jax.sharding import PartitionSpec as P

HB = 128
ITERS = 2
BLOCK = 256
F32 = jnp.float32
BF16 = jnp.bfloat16

precise = lax.Precision.HIGHEST
NT = (((1,), (1,)), ((), ()))
NN = (((1,), (0,)), ((), ()))
VMEM = pl.BlockSpec(memory_space=pltpu.VMEM)
SMEM = pl.BlockSpec(memory_space=pltpu.SMEM)


def dot(a, b, dims):
    return lax.dot_general(a, b, dims, preferred_element_type=F32)


def exact(a, b, dims):
    return lax.dot_general(a, b, dims, precision=precise, preferred_element_type=F32)


def split(values):
    high = values.astype(BF16)
    return high, (values - high.astype(F32)).astype(BF16)


def sign_table(order):
    row = lax.broadcasted_iota(jnp.int32, (order, order), 0)
    common = row & lax.broadcasted_iota(jnp.int32, (order, order), 1)
    parity = common
    shift = 16
    while shift:
        parity = parity ^ (parity >> shift)
        shift //= 2
    return (1 - 2 * (parity & 1)).astype(F32)


def butterfly(ref, count):
    rows = ref.shape[0]
    step = 1
    while step < count:
        radix = min(8, count // step)

        def body(g, carry, step=step, radix=radix):
            base = (g // step) * (step * radix) + g % step
            for s in range(rows // 8):
                at = [pl.multiple_of((base + r * step) * HB, HB) for r in range(radix)]
                v = [ref[s * 8 : s * 8 + 8, pl.ds(a, HB)] for a in at]
                half = 1
                while half < radix:
                    v = [
                        v[r] + v[r + half] if not r & half else v[r - half] - v[r]
                        for r in range(radix)
                    ]
                    half *= 2
                for a, x in zip(at, v):
                    ref[s * 8 : s * 8 + 8, pl.ds(a, HB)] = x
            return carry

        lax.fori_loop(0, count // radix, body, 0)
        step *= radix


def block_loop(count, unroll, body):
    unroll = math.gcd(count, unroll)

    def many(i, carry):
        for q in range(unroll):
            body(i * unroll + q)
        return carry

    lax.fori_loop(0, count // unroll, many, 0)


def start_kernel(
    scale, idx_ref, at_ref, probes_ref, frames_ref, dh_ref, dl_ref, img_ref,
    f_ref, w_ref, n_ref, g_ref, b_ref, t_ref, sems,
):
    vectors, modes = probes_ref.shape
    rows, count = frames_ref.shape[1:]
    outer = modes // HB
    block = min(BLOCK, rows)
    copies = [
        [
            pltpu.make_async_copy(
                frames_ref.at[s, pl.ds(i * block, block)],
                f_ref.at[s, pl.ds(i * block, block)],
                sems.at[s, i],
            )
            for s in range(frames_ref.shape[0])
        ]
        for i in range(rows // block)
    ]
    for row in copies:
        for c in row:
            c.start()
    signs = sign_table(HB).astype(BF16)

    def inner(i):
        at = pl.multiple_of(i * HB, HB)
        both = dot(jnp.concatenate(split(probes_ref[:, pl.ds(at, HB)]), axis=0), signs, NN)
        w_ref[:, pl.ds(at, HB)] = both[:vectors] + both[vectors:]

    block_loop(outer, 8, inner)
    butterfly(w_ref, outer)

    def turn(i):
        at = pl.multiple_of(i * HB, HB)
        here = w_ref[:, pl.ds(at, HB)]
        n_ref[pl.ds(at, HB), :] = jnp.concatenate([here, here], axis=0).T

    block_loop(outer, 8, turn)

    def gather(t, carry):
        at = pl.multiple_of(t * 8, 8)
        for q in range(8):
            g_ref[pl.ds(at + q, 1), :] = n_ref[pl.ds(idx_ref[at + q], 1), :]
        return carry

    lax.fori_loop(0, count // 8, gather, 0)
    parts = [g_ref[b * HB : (b + 1) * HB, :].T[:vectors] for b in range(count // HB)]
    b_ref[...], t_ref[...] = stack_forward(jnp.concatenate(parts, axis=1) * scale)
    for i, row in enumerate(copies):
        for c in row:
            c.wait()
        span = slice(i * block, (i + 1) * block)
        for part in (0, 1):
            high, low = split(0.25 * (f_ref[at_ref[part], span] - f_ref[at_ref[part + 2], span]))
            dh_ref[part, span] = high
            dl_ref[part, span] = low
        img_ref[:, span] = apply_forward(b_ref[...], t_ref[...], dh_ref, dl_ref, span)


def start(idx, steps_at, probes, frames, scale):
    vectors, modes = probes.shape
    steps, rows, count = frames.shape
    planes = jax.ShapeDtypeStruct((2, rows, count), BF16)
    return pl.pallas_call(
        functools.partial(start_kernel, scale),
        out_shape=[planes, planes, jax.ShapeDtypeStruct((vectors, rows), F32)],
        in_specs=[SMEM, SMEM, VMEM, pl.BlockSpec(memory_space=pltpu.HBM)],
        out_specs=[VMEM, VMEM, VMEM],
        scratch_shapes=[
            pltpu.VMEM((steps, rows, count), F32),
            pltpu.VMEM((vectors, modes), F32),
            pltpu.VMEM((modes, HB), F32),
            pltpu.VMEM((count, HB), F32),
            pltpu.VMEM((2 * vectors, count), BF16),
            pltpu.VMEM((2 * vectors, count), BF16),
            pltpu.SemaphoreType.DMA((steps, rows // min(BLOCK, rows))),
        ],
        compiler_params=pltpu.CompilerParams(vmem_limit_bytes=44 << 20),
    )(idx, steps_at, probes, frames)


def scatter_kernel(base_ref, idx_ref, *refs):
    s_ref, w_ref = refs[-1], refs[-2]
    pieces = [r for r in refs[:-2] if len(r.shape) == 2 and r.shape[1] == s_ref.shape[0]]
    count = s_ref.shape[0]
    for p, x_ref in enumerate(pieces):
        for i in range(count // HB):
            high, low = split(x_ref[:, i * HB : (i + 1) * HB])
            both = jnp.concatenate([high.astype(F32), low.astype(F32)], axis=0)
            s_ref[i * HB : (i + 1) * HB, :] = both.T
        base = base_ref[p]

        def move(t, carry, base=base):
            at = pl.multiple_of(t * 16, 16)
            for q in range(16):
                w_ref[pl.ds(idx_ref[base + at + q], 1), :] = s_ref[pl.ds(at + q, 1), :]
            return carry

        lax.fori_loop(0, count // 16, move, 0)


def scatter_rows(bases, idx, pieces, table=None):
    count = pieces[0].shape[1]
    args = [bases, idx, *pieces] + ([] if table is None else [table])
    return pl.pallas_call(
        scatter_kernel,
        out_shape=jax.ShapeDtypeStruct((idx.shape[0], HB), F32),
        in_specs=[SMEM, SMEM] + [VMEM] * (len(args) - 2),
        out_specs=VMEM,
        scratch_shapes=[pltpu.VMEM((count, HB), F32)],
        input_output_aliases={} if table is None else {len(args) - 1: 0},
        compiler_params=pltpu.CompilerParams(vmem_limit_bytes=8 << 20),
    )(*args)


def end_kernel(inv_ref, w_ref, out_ref):
    vectors, modes = out_ref.shape
    half = vectors // 2
    outer = modes // HB
    signs = sign_table(HB).astype(BF16)
    zero = jnp.zeros((half, half), F32)
    wide = jnp.concatenate(
        [jnp.concatenate([inv_ref[...], zero], 1), jnp.concatenate([zero, inv_ref[...]], 1)], 0
    )
    high, low = split(wide)
    mix = jnp.concatenate(
        [jnp.concatenate([high, high], 1), jnp.concatenate([low, jnp.zeros_like(low)], 1)], 0
    )

    def first(i):
        at = pl.multiple_of(i * HB, HB)
        both = dot(mix, w_ref[pl.ds(at, HB), :].astype(BF16), NT)
        out_ref[:, pl.ds(at, HB)] = both[:vectors] + both[vectors:]

    block_loop(outer, 8, first)
    butterfly(out_ref, outer)

    def inner(i):
        at = pl.multiple_of(i * HB, HB)
        both = dot(jnp.concatenate(split(out_ref[:, pl.ds(at, HB)]), axis=0), signs, NN)
        out_ref[:, pl.ds(at, HB)] = both[:vectors] + both[vectors:]

    block_loop(outer, 8, inner)


def end_vectors(inv, table, vectors):
    return pl.pallas_call(
        end_kernel,
        out_shape=jax.ShapeDtypeStruct((vectors, table.shape[0]), F32),
        in_specs=[VMEM, VMEM],
        out_specs=VMEM,
        compiler_params=pltpu.CompilerParams(vmem_limit_bytes=12 << 20),
    )(inv, table)


def factor_kernel(g_ref, out_ref):
    n = g_ref.shape[0]
    row = lax.broadcasted_iota(jnp.int32, (n, n), 0)
    eye = (row == lax.broadcasted_iota(jnp.int32, (n, n), 1)).astype(F32)
    both = jnp.concatenate([g_ref[...], eye], axis=1)
    below = lax.broadcasted_iota(jnp.int32, (n, 1), 0)
    for k in range(n - 1):
        scaled = both[k : k + 1] * (1.0 / both[k : k + 1, k : k + 1])
        both = both - jnp.where(below > k, both[:, k : k + 1], 0.0) * scaled
    pivots = jnp.sum(both[:, :n] * eye, axis=1, keepdims=True)
    out_ref[...] = both[:, n:] * (1.0 / jnp.sqrt(pivots))


def inverse_factor(gram_matrix):
    return pl.pallas_call(
        factor_kernel,
        out_shape=jax.ShapeDtypeStruct(gram_matrix.shape, F32),
        in_specs=[VMEM],
        out_specs=VMEM,
        compiler_params=pltpu.CompilerParams(vmem_limit_bytes=2 << 20),
    )(gram_matrix)


def stack_forward(u):
    half = u.shape[0] // 2
    turned = jnp.concatenate([-u[half:], u[:half]], axis=0)
    uh, ul = split(u)
    th, tl = split(turned)
    return jnp.concatenate([uh, ul], axis=0), jnp.concatenate([th, tl], axis=0)


def apply_forward(both, turned, dh, dl, span):
    n = both.shape[0] // 2
    wide = dot(both, dh[0, span], NT) + dot(turned, dh[1, span], NT)
    low = dot(both[:n], dl[0, span], NT) + dot(turned[:n], dl[1, span], NT)
    return wide[:n] + wide[n:] + low


def forward_kernel(u_ref, dh_ref, dl_ref, img_ref):
    both, turned = stack_forward(u_ref[...])
    rows = dh_ref.shape[1]
    block = min(BLOCK, rows)
    width = img_ref.shape[-1]
    for i in range(rows // block):
        part = apply_forward(both, turned, dh_ref, dl_ref, slice(i * block, (i + 1) * block))
        if len(img_ref.shape) == 2:
            img_ref[:, i * block : (i + 1) * block] = part
        else:
            for j in range(block // width):
                img_ref[i * block // width + j] = part[:, j * width : (j + 1) * width]


def forward(u, dh, dl, places=None):
    rows = dh.shape[1]
    vectors = u.shape[0]
    shape = (vectors, rows) if places is None else (places, vectors, rows // places)
    return pl.pallas_call(
        forward_kernel,
        out_shape=jax.ShapeDtypeStruct(shape, F32),
        in_specs=[VMEM, VMEM, VMEM],
        out_specs=VMEM,
        compiler_params=pltpu.CompilerParams(vmem_limit_bytes=12 << 20),
    )(u, dh, dl)


def backward_kernel(*refs):
    inv_ref = refs[0] if len(refs) == 5 else None
    img_ref, dh_ref, dl_ref, ret_ref = refs[-4:]
    vectors, rows = img_ref.shape
    half = vectors // 2
    real, imag = img_ref[:half], img_ref[half:]
    if inv_ref is not None:
        real = exact(inv_ref[...], real, NN)
        imag = exact(inv_ref[...], imag, NN)
    stacks = []
    for pair in ([real, imag], [imag, -real]):
        high, low = split(jnp.concatenate(pair, axis=0))
        stacks.append((high, jnp.concatenate([high, low], axis=0)))
    cols = dh_ref.shape[2]
    block = min(BLOCK, cols)
    for i in range(cols // block):
        span = slice(i * block, (i + 1) * block)
        wide = dot(stacks[0][1], dh_ref[0, :, span], NN) + dot(stacks[1][1], dh_ref[1, :, span], NN)
        low = dot(stacks[0][0], dl_ref[0, :, span], NN) + dot(stacks[1][0], dl_ref[1, :, span], NN)
        ret_ref[:, span] = wide[:vectors] + wide[vectors:] + low


def backward(inv, images, dh, dl):
    args = ([] if inv is None else [inv]) + [images, dh, dl]
    return pl.pallas_call(
        backward_kernel,
        out_shape=jax.ShapeDtypeStruct((images.shape[0], dh.shape[2]), F32),
        in_specs=[VMEM] * len(args),
        out_specs=VMEM,
        compiler_params=pltpu.CompilerParams(vmem_limit_bytes=12 << 20),
    )(*args)


def gram(vectors):
    half = vectors.shape[0] // 2
    return exact(vectors[:half], vectors[:half], NT) + exact(vectors[half:], vectors[half:], NT)


def normalise(inv, vectors):
    half = inv.shape[0]
    return jnp.concatenate([exact(inv, vectors[:half], NN), exact(inv, vectors[half:], NN)], axis=0)


def flip(n, bit):
    return [(i, i ^ bit) for i in range(n)]


def pick(pieces, here, n):
    bit = 1
    while bit < n:
        odd = (here & bit) != 0
        pieces = [jnp.where(odd, pieces[b ^ bit], pieces[b]) for b in range(n)]
        bit *= 2
    return pieces


def scatter_sum(blocks, axis, step, n):
    size = lax.axis_size(axis)
    here = (lax.axis_index(axis) // step) % n
    mine = pick(blocks, here, n)
    total = mine[0]
    for b in range(1, n):
        total = total + lax.ppermute(mine[b], axis, flip(size, b * step))
    return total


def gather_all(block, axis, step, n):
    size = lax.axis_size(axis)
    here = (lax.axis_index(axis) // step) % n
    pieces = [block] + [lax.ppermute(block, axis, flip(size, b * step)) for b in range(1, n)]
    return pick(pieces, here, n)


def share_sum(block, axis, step, n):
    size = lax.axis_size(axis)
    total = block
    for b in range(1, n):
        total = total + lax.ppermute(block, axis, flip(size, b * step))
    return total


def double_sum(block, axis):
    size = lax.axis_size(axis)
    bit = 1
    while bit < size:
        block = block + lax.ppermute(block, axis, flip(size, bit))
        bit *= 2
    return block


def sum_pix(x):
    n = lax.axis_size("pix")
    if n != 4:
        return double_sum(x, "pix")
    rows = x.shape[0] // n
    mine = scatter_sum([x[i * rows : (i + 1) * rows] for i in range(n)], "pix", 1, n)
    return jnp.concatenate(gather_all(mine, "pix", 1, n), axis=0)


def pack(gram_matrix, width):
    return jnp.pad(gram_matrix.reshape(1, -1), ((0, 7), (0, width - gram_matrix.size)))


def sum_mode(x, extra=None):
    n = lax.axis_size("mode")
    rows, cols = x.shape
    if n != 8:
        total = double_sum(x, "mode")
        return total, (None if extra is None else double_sum(extra, "mode"))
    half = rows // 2
    odd = (lax.axis_index("mode") % 2) != 0
    mine = jnp.where(odd, x[half:], x[:half])
    other = jnp.where(odd, x[:half], x[half:])
    if extra is not None:
        k = extra.shape[0]
        row = pack(extra, cols)
        mine = jnp.concatenate([mine, row], axis=0)
        other = jnp.concatenate([other, row], axis=0)
    chip = mine + lax.ppermute(other, "mode", flip(n, 1))
    chip = share_sum(chip, "mode", 2, 4)
    mine = chip[:half]
    other = lax.ppermute(mine, "mode", flip(n, 1))
    total = jnp.concatenate([jnp.where(odd, other, mine), jnp.where(odd, mine, other)], axis=0)
    if extra is None:
        return total, None
    return total, chip[half, : k * k].reshape(k, k)


def scatter_mode(pieces, extra):
    places, rows, width = pieces.shape
    k = extra.shape[0]
    n = lax.axis_size("mode")
    here = lax.axis_index("mode")
    if n != 8:
        total = double_sum(pieces, "mode")
        return lax.dynamic_index_in_dim(total, here, 0, False), double_sum(extra, "mode")
    chips = pieces.reshape(4, 2, rows, width)
    odd = (here % 2) != 0
    mine = jnp.where(odd, chips[:, 1], chips[:, 0]).reshape(4 * rows, width)
    other = jnp.where(odd, chips[:, 0], chips[:, 1]).reshape(4 * rows, width)
    small = extra.reshape(k * k // width, width)
    got = lax.ppermute(jnp.concatenate([other, small], axis=0), "mode", flip(n, 1))
    mine = mine + got[: 4 * rows]
    small = small + got[4 * rows :]
    blocks = [
        jnp.concatenate([mine[i * rows : (i + 1) * rows], small], axis=0) for i in range(4)
    ]
    total = scatter_sum(blocks, "mode", 2, 4)
    return total[:rows], total[rows:].reshape(k, k)


def gather_rows(block, idx):
    n = lax.axis_size("mode")
    here = lax.axis_index("mode")
    count = block.shape[1]

    def bases(bits):
        return jnp.stack([(here ^ b) * count for b in bits]).astype(jnp.int32)

    if n != 8:
        pieces = [block]
        bit = 1
        while bit < n:
            pieces = pieces + [lax.ppermute(p, "mode", flip(n, bit)) for p in pieces]
            bit *= 2
        return scatter_rows(bases(range(n)), idx, pieces)
    far = {b: lax.ppermute(block, "mode", flip(n, b)) for b in (2, 4, 6)}
    near = lax.ppermute(block, "mode", flip(n, 1))
    table = scatter_rows(bases((0, 1)), idx, [block, near])
    for b in (2, 4, 6):
        other = lax.ppermute(far[b], "mode", flip(n, 1))
        table = scatter_rows(bases((b, b ^ 1)), idx, [far[b], other], table)
    return table


def local(frames, phase_steps, pattern_rows, probes):
    columns = frames.shape[2]
    rows = frames.shape[1]
    groups = lax.axis_size("mode")
    pixels = rows * lax.axis_size("pix")
    modes_total = columns * groups
    k = probes.shape[1]
    vectors = 2 * k
    probes = probes.reshape(vectors, modes_total)
    here = lax.axis_index("mode")
    steps_at = jnp.sum(
        jnp.where(phase_steps[None, :] == jnp.arange(4)[:, None], jnp.arange(4)[None, :], 0), axis=1
    ).astype(jnp.int32)
    my_rows = lax.dynamic_slice_in_dim(pattern_rows, here * columns, columns)
    dh, dl, images = start(my_rows, steps_at, probes, frames, 1.0 / math.sqrt(modes_total))
    inv = inverse_factor(gram(probes))
    images, _ = sum_mode(images)
    returned = sum_pix(backward(inv, images, dh, dl))
    for iteration in range(1, ITERS):
        images, gram_matrix = sum_mode(forward(returned, dh, dl), gram(returned))
        inv = inverse_factor(gram_matrix)
        returned = normalise(inv, sum_pix(backward(None, images, dh, dl)))
    table = gather_rows(returned, pattern_rows)
    fields, gram_matrix = scatter_mode(forward(returned, dh, dl, groups), gram(returned))
    inv = inverse_factor(gram_matrix)
    fields = normalise(inv, fields)
    power = jnp.sum(fields * fields, axis=1)
    power = jnp.broadcast_to((power[:k] + power[k:])[None, :], (8, k))
    power = double_sum(double_sum(power, "mode"), "pix")
    strengths = power[0] / pixels
    channels = end_vectors(inv, table, vectors)
    return (channels.reshape(2, k, modes_total), fields.reshape(2, k, -1), strengths)


def solution(mesh):
    in_specs = (P(None, "pix", "mode"), P(), P(), P())
    out_specs = (P(), P(None, None, ("pix", "mode")), P())
    return jax.shard_map(local, mesh=mesh, in_specs=in_specs, out_specs=out_specs, check_vma=False)
```

```python
import functools
import math

import jax
import jax.numpy as jnp
from jax import lax
from jax.experimental import pallas as pl
from jax.experimental.pallas import tpu as pltpu
from jax.sharding import PartitionSpec as P

HB = 128
ITERS = 2
BLOCK = 256
F32 = jnp.float32
BF16 = jnp.bfloat16

precise = lax.Precision.HIGHEST
NT = (((1,), (1,)), ((), ()))
NN = (((1,), (0,)), ((), ()))
VMEM = pl.BlockSpec(memory_space=pltpu.VMEM)
SMEM = pl.BlockSpec(memory_space=pltpu.SMEM)


def dot(a, b, dims):
    return lax.dot_general(a, b, dims, preferred_element_type=F32)


def exact(a, b, dims):
    return lax.dot_general(a, b, dims, precision=precise, preferred_element_type=F32)


def in_vmem(x):
    return pltpu.with_memory_space_constraint(x, pltpu.VMEM)


def split(values):
    high = values.astype(BF16)
    return high, (values - high.astype(F32)).astype(BF16)


def sign_table(order):
    row = lax.broadcasted_iota(jnp.int32, (order, order), 0)
    common = row & lax.broadcasted_iota(jnp.int32, (order, order), 1)
    parity = common
    shift = 16
    while shift:
        parity = parity ^ (parity >> shift)
        shift //= 2
    return (1 - 2 * (parity & 1)).astype(F32)


def butterfly(ref, count):
    rows = ref.shape[0]
    step = 1
    while step < count:
        radix = min(8, count // step)

        def body(g, carry, step=step, radix=radix):
            base = (g // step) * (step * radix) + g % step
            for s in range(rows // 8):
                at = [pl.multiple_of((base + r * step) * HB, HB) for r in range(radix)]
                v = [ref[s * 8 : s * 8 + 8, pl.ds(a, HB)] for a in at]
                half = 1
                while half < radix:
                    v = [
                        v[r] + v[r + half] if not r & half else v[r - half] - v[r]
                        for r in range(radix)
                    ]
                    half *= 2
                for a, x in zip(at, v):
                    ref[s * 8 : s * 8 + 8, pl.ds(a, HB)] = x
            return carry

        lax.fori_loop(0, count // radix, body, 0)
        step *= radix


def block_loop(count, unroll, body):
    unroll = math.gcd(count, unroll)

    def many(i, carry):
        for q in range(unroll):
            body(i * unroll + q)
        return carry

    lax.fori_loop(0, count // unroll, many, 0)


def start_kernel(
    scale, here_ref, idx_ref, at_ref, probes_ref, frames_ref,
    dh_ref, dl_ref, img_ref, mask_ref, base_ref, f_ref, w_ref, n_ref, g_ref, b_ref, t_ref, sems,
):
    vectors, modes = probes_ref.shape
    rows, count = frames_ref.shape[1:]
    outer = modes // HB
    block = min(BLOCK, rows)
    copies = [
        [
            pltpu.make_async_copy(
                frames_ref.at[s, pl.ds(i * block, block)],
                f_ref.at[s, pl.ds(i * block, block)],
                sems.at[s, i],
            )
            for s in range(frames_ref.shape[0])
        ]
        for i in range(rows // block)
    ]
    for row in copies:
        for c in row:
            c.start()
    for b in range(4):
        for place, axis_row in ((here_ref[0], 0), (here_ref[1], 4)):
            bit = ((place >> b) & 1).astype(F32)
            mask_ref[axis_row + b : axis_row + b + 1, :] = jnp.full((1, HB), bit, F32)
    for b in range(base_ref.shape[0]):
        base_ref[b] = (here_ref[0] ^ b) * count
    signs = sign_table(HB).astype(BF16)

    def inner(i):
        at = pl.multiple_of(i * HB, HB)
        both = dot(jnp.concatenate(split(probes_ref[:, pl.ds(at, HB)]), axis=0), signs, NN)
        w_ref[:, pl.ds(at, HB)] = both[:vectors] + both[vectors:]

    block_loop(outer, 8, inner)
    butterfly(w_ref, outer)

    def turn(i):
        at = pl.multiple_of(i * HB, HB)
        here = w_ref[:, pl.ds(at, HB)]
        n_ref[pl.ds(at, HB), :] = jnp.concatenate([here, here], axis=0).T

    block_loop(outer, 8, turn)

    def gather(t, carry):
        at = pl.multiple_of(t * 8, 8)
        for q in range(8):
            g_ref[pl.ds(at + q, 1), :] = n_ref[pl.ds(idx_ref[at + q], 1), :]
        return carry

    lax.fori_loop(0, count // 8, gather, 0)
    parts = [g_ref[b * HB : (b + 1) * HB, :].T[:vectors] for b in range(count // HB)]
    b_ref[...], t_ref[...] = stack_forward(jnp.concatenate(parts, axis=1) * scale)
    for i, row in enumerate(copies):
        for c in row:
            c.wait()
        span = slice(i * block, (i + 1) * block)
        for part in (0, 1):
            high, low = split(0.25 * (f_ref[at_ref[part], span] - f_ref[at_ref[part + 2], span]))
            dh_ref[part, span] = high
            dl_ref[part, span] = low
        img_ref[:, span] = apply_forward(b_ref[...], t_ref[...], dh_ref, dl_ref, span)


def cost(us):
    return pl.CostEstimate(flops=0, transcendentals=0, bytes_accessed=int(us * 3.5e6))


def start(here, idx, steps_at, probes, frames, scale):
    vectors, modes = probes.shape
    steps, rows, count = frames.shape
    planes = pltpu.VMEM((2, rows, count), BF16)
    return pl.pallas_call(
        functools.partial(start_kernel, scale),
        out_shape=[
            planes,
            planes,
            jax.ShapeDtypeStruct((vectors, rows), F32),
            jax.ShapeDtypeStruct((8, HB), F32),
            jax.ShapeDtypeStruct((modes // count,), jnp.int32),
        ],
        in_specs=[SMEM, SMEM, SMEM, VMEM, pl.BlockSpec(memory_space=pltpu.HBM)],
        out_specs=[VMEM, VMEM, VMEM, VMEM, SMEM],
        cost_estimate=cost(12),
        scratch_shapes=[
            pltpu.VMEM((steps, rows, count), F32),
            pltpu.VMEM((vectors, modes), F32),
            pltpu.VMEM((modes, HB), F32),
            pltpu.VMEM((count, HB), F32),
            pltpu.VMEM((2 * vectors, count), BF16),
            pltpu.VMEM((2 * vectors, count), BF16),
            pltpu.SemaphoreType.DMA((steps, rows // min(BLOCK, rows))),
        ],
        compiler_params=pltpu.CompilerParams(vmem_limit_bytes=44 << 20),
    )(here, idx, steps_at, probes, frames)


def scatter_kernel(places, base_ref, idx_ref, *refs):
    s_ref, w_ref = refs[-1], refs[-2]
    pieces = [r for r in refs[:-2] if len(r.shape) == 2 and r.shape[1] == s_ref.shape[0]]
    count = s_ref.shape[0]
    for p, x_ref in enumerate(pieces):
        for i in range(count // HB):
            high, low = split(x_ref[:, i * HB : (i + 1) * HB])
            both = jnp.concatenate([high.astype(F32), low.astype(F32)], axis=0)
            s_ref[i * HB : (i + 1) * HB, :] = both.T
        base = base_ref[places[p]]

        def move(t, carry, base=base):
            at = pl.multiple_of(t * 16, 16)
            for q in range(16):
                w_ref[pl.ds(idx_ref[base + at + q], 1), :] = s_ref[pl.ds(at + q, 1), :]
            return carry

        lax.fori_loop(0, count // 16, move, 0)


def scatter_rows(places, bases, idx, pieces, table=None):
    count = pieces[0].shape[1]
    args = [bases, idx, *pieces] + ([] if table is None else [table])
    return pl.pallas_call(
        functools.partial(scatter_kernel, places),
        cost_estimate=cost(1.7 * len(pieces)),
        out_shape=jax.ShapeDtypeStruct((idx.shape[0], HB), F32),
        in_specs=[SMEM, SMEM] + [VMEM] * (len(args) - 2),
        out_specs=VMEM,
        scratch_shapes=[pltpu.VMEM((count, HB), F32)],
        input_output_aliases={} if table is None else {len(args) - 1: 0},
        compiler_params=pltpu.CompilerParams(vmem_limit_bytes=8 << 20),
    )(*args)


def end_kernel(inv_ref, w_ref, out_ref):
    vectors, modes = out_ref.shape
    half = vectors // 2
    outer = modes // HB
    signs = sign_table(HB).astype(BF16)
    zero = jnp.zeros((half, half), F32)
    wide = jnp.concatenate(
        [jnp.concatenate([inv_ref[...], zero], 1), jnp.concatenate([zero, inv_ref[...]], 1)], 0
    )
    high, low = split(wide)
    mix = jnp.concatenate(
        [jnp.concatenate([high, high], 1), jnp.concatenate([low, jnp.zeros_like(low)], 1)], 0
    )

    def first(i):
        at = pl.multiple_of(i * HB, HB)
        both = dot(mix, w_ref[pl.ds(at, HB), :].astype(BF16), NT)
        out_ref[:, pl.ds(at, HB)] = both[:vectors] + both[vectors:]

    block_loop(outer, 8, first)
    butterfly(out_ref, outer)

    def inner(i):
        at = pl.multiple_of(i * HB, HB)
        both = dot(jnp.concatenate(split(out_ref[:, pl.ds(at, HB)]), axis=0), signs, NN)
        out_ref[:, pl.ds(at, HB)] = both[:vectors] + both[vectors:]

    block_loop(outer, 8, inner)


def end_vectors(inv, table, vectors):
    return pl.pallas_call(
        end_kernel,
        cost_estimate=cost(12),
        out_shape=jax.ShapeDtypeStruct((vectors, table.shape[0]), F32),
        in_specs=[VMEM, VMEM],
        out_specs=VMEM,
        compiler_params=pltpu.CompilerParams(vmem_limit_bytes=12 << 20),
    )(inv, table)


def factor_kernel(g_ref, out_ref):
    n = out_ref.shape[0]
    square = jnp.concatenate([g_ref[:, i * n : (i + 1) * n] for i in range(n // 8)], axis=0)
    row = lax.broadcasted_iota(jnp.int32, (n, n), 0)
    eye = (row == lax.broadcasted_iota(jnp.int32, (n, n), 1)).astype(F32)
    both = jnp.concatenate([square, eye], axis=1)
    below = lax.broadcasted_iota(jnp.int32, (n, 1), 0)
    for k in range(n - 1):
        scaled = both[k : k + 1] * (1.0 / both[k : k + 1, k : k + 1])
        both = both - jnp.where(below > k, both[:, k : k + 1], 0.0) * scaled
    pivots = jnp.sum(both[:, :n] * eye, axis=1, keepdims=True)
    out_ref[...] = both[:, n:] * (1.0 / jnp.sqrt(pivots))


def pack(gram_matrix):
    n = gram_matrix.shape[0]
    return jnp.concatenate([gram_matrix[i : i + 8] for i in range(0, n, 8)], axis=1)


def inverse_factor(packed, n):
    return pl.pallas_call(
        factor_kernel,
        cost_estimate=cost(2.7),
        out_shape=jax.ShapeDtypeStruct((n, n), F32),
        in_specs=[VMEM],
        out_specs=VMEM,
        compiler_params=pltpu.CompilerParams(vmem_limit_bytes=2 << 20),
    )(packed)


def stack_forward(u):
    half = u.shape[0] // 2
    turned = jnp.concatenate([-u[half:], u[:half]], axis=0)
    uh, ul = split(u)
    th, tl = split(turned)
    return jnp.concatenate([uh, ul], axis=0), jnp.concatenate([th, tl], axis=0)


def apply_forward(both, turned, dh, dl, span):
    n = both.shape[0] // 2
    wide = dot(both, dh[0, span], NT) + dot(turned, dh[1, span], NT)
    low = dot(both[:n], dl[0, span], NT) + dot(turned[:n], dl[1, span], NT)
    return wide[:n] + wide[n:] + low


def gram(vectors):
    half = vectors.shape[0] // 2
    return exact(vectors[:half], vectors[:half], NT) + exact(vectors[half:], vectors[half:], NT)


def forward_kernel(u_ref, dh_ref, dl_ref, img_ref, gram_ref):
    gram_ref[...] = pack(gram(u_ref[...]))
    both, turned = stack_forward(u_ref[...])
    rows = dh_ref.shape[1]
    block = min(BLOCK, rows)
    width = img_ref.shape[-1]
    for i in range(rows // block):
        part = apply_forward(both, turned, dh_ref, dl_ref, slice(i * block, (i + 1) * block))
        if len(img_ref.shape) == 2:
            img_ref[:, i * block : (i + 1) * block] = part
        else:
            for j in range(block // width):
                img_ref[i * block // width + j] = part[:, j * width : (j + 1) * width]


def forward(u, dh, dl, places=None):
    rows = dh.shape[1]
    vectors = u.shape[0]
    shape = (vectors, rows) if places is None else (places, vectors, rows // places)
    return pl.pallas_call(
        forward_kernel,
        out_shape=[
            jax.ShapeDtypeStruct(shape, F32),
            jax.ShapeDtypeStruct((8, vectors // 2 * vectors // 16), F32),
        ],
        in_specs=[VMEM, VMEM, VMEM],
        out_specs=[VMEM, VMEM],
        cost_estimate=cost(2.7),
        compiler_params=pltpu.CompilerParams(vmem_limit_bytes=12 << 20),
    )(u, in_vmem(dh), in_vmem(dl))


def backward_kernel(*refs):
    inv_ref = refs[0] if len(refs) == 5 else None
    img_ref, dh_ref, dl_ref, ret_ref = refs[-4:]
    vectors, rows = img_ref.shape
    half = vectors // 2
    real, imag = img_ref[:half], img_ref[half:]
    if inv_ref is not None:
        real = exact(inv_ref[...], real, NN)
        imag = exact(inv_ref[...], imag, NN)
    stacks = []
    for pair in ([real, imag], [imag, -real]):
        high, low = split(jnp.concatenate(pair, axis=0))
        stacks.append((high, jnp.concatenate([high, low], axis=0)))
    cols = dh_ref.shape[2]
    block = min(BLOCK, cols)
    for i in range(cols // block):
        span = slice(i * block, (i + 1) * block)
        wide = dot(stacks[0][1], dh_ref[0, :, span], NN) + dot(stacks[1][1], dh_ref[1, :, span], NN)
        low = dot(stacks[0][0], dl_ref[0, :, span], NN) + dot(stacks[1][0], dl_ref[1, :, span], NN)
        ret_ref[:, span] = wide[:vectors] + wide[vectors:] + low


def backward(inv, images, dh, dl):
    args = ([] if inv is None else [inv]) + [images, in_vmem(dh), in_vmem(dl)]
    return pl.pallas_call(
        backward_kernel,
        cost_estimate=cost(1.6),
        out_shape=jax.ShapeDtypeStruct((images.shape[0], dh.shape[2]), F32),
        in_specs=[VMEM] * len(args),
        out_specs=VMEM,
        compiler_params=pltpu.CompilerParams(vmem_limit_bytes=12 << 20),
    )(*args)


def normalise(inv, vectors):
    half = inv.shape[0]
    return jnp.concatenate([exact(inv, vectors[:half], NN), exact(inv, vectors[half:], NN)], axis=0)


def flip(n, bit):
    return [(i, i ^ bit) for i in range(n)]


def pick(pieces, odds):
    for bit, odd in enumerate(odds):
        pieces = [jnp.where(odd, pieces[b ^ (1 << bit)], pieces[b]) for b in range(len(pieces))]
    return pieces


def scatter_sum(blocks, axis, step, odds):
    size = lax.axis_size(axis)
    mine = pick(blocks, odds)
    total = mine[0]
    for b in range(1, len(blocks)):
        total = total + lax.ppermute(mine[b], axis, flip(size, b * step))
    return total


def gather_all(block, axis, step, odds):
    size = lax.axis_size(axis)
    far = [lax.ppermute(block, axis, flip(size, b * step)) for b in range(1, 2 ** len(odds))]
    return pick([block] + far, odds)


def share_sum(block, axis, step, n):
    size = lax.axis_size(axis)
    total = block
    for b in range(1, n):
        total = total + lax.ppermute(block, axis, flip(size, b * step))
    return total


def double_sum(block, axis):
    size = lax.axis_size(axis)
    bit = 1
    while bit < size:
        block = block + lax.ppermute(block, axis, flip(size, bit))
        bit *= 2
    return block


def sum_pix(x, odds):
    n = lax.axis_size("pix")
    if n != 4:
        return double_sum(x, "pix")
    rows = x.shape[0] // n
    odds = odds[4:6]
    mine = scatter_sum([x[i * rows : (i + 1) * rows] for i in range(n)], "pix", 1, odds)
    return jnp.concatenate(gather_all(mine, "pix", 1, odds), axis=0)


def sum_mode(x, odds, extra=None):
    n = lax.axis_size("mode")
    rows, cols = x.shape
    if n != 8:
        return double_sum(x, "mode"), (None if extra is None else double_sum(extra, "mode"))
    half = rows // 2
    odd = odds[0]
    mine = jnp.where(odd, x[half:], x[:half])
    other = jnp.where(odd, x[:half], x[half:])
    if extra is not None:
        width = extra.shape[1]
        row = jnp.pad(extra, ((0, 0), (0, cols - width)))
        mine = jnp.concatenate([mine, row], axis=0)
        other = jnp.concatenate([other, row], axis=0)
    chip = mine + lax.ppermute(other, "mode", flip(n, 1))
    chip = share_sum(chip, "mode", 2, 4)
    mine = chip[:half]
    other = lax.ppermute(mine, "mode", flip(n, 1))
    total = jnp.concatenate([jnp.where(odd, other, mine), jnp.where(odd, mine, other)], axis=0)
    return total, (None if extra is None else chip[half:, :width])


def scatter_mode(pieces, odds, extra):
    places, rows, width = pieces.shape
    n = lax.axis_size("mode")
    here = lax.axis_index("mode")
    if n != 8:
        total = double_sum(pieces, "mode")
        return lax.dynamic_index_in_dim(total, here, 0, False), double_sum(extra, "mode")
    odd = odds[0]
    mine = jnp.concatenate([jnp.where(odd, pieces[2 * i + 1], pieces[2 * i]) for i in range(4)])
    other = [jnp.where(odd, pieces[2 * i], pieces[2 * i + 1]) for i in range(4)]
    small = jnp.pad(extra, ((0, 0), (0, width - extra.shape[1])))
    got = lax.ppermute(jnp.concatenate(other + [small], axis=0), "mode", flip(n, 1))
    mine = mine + got[: 4 * rows]
    small = small + got[4 * rows :]
    blocks = [
        jnp.concatenate([mine[i * rows : (i + 1) * rows], small], axis=0) for i in range(4)
    ]
    total = scatter_sum(blocks, "mode", 2, odds[1:3])
    return total[:rows], total[rows:, : extra.shape[1]]


def gather_rows(block, bases, idx):
    n = lax.axis_size("mode")
    if n != 8:
        pieces = [block]
        bit = 1
        while bit < n:
            pieces = pieces + [lax.ppermute(p, "mode", flip(n, bit)) for p in pieces]
            bit *= 2
        return scatter_rows(range(n), bases, idx, pieces)
    near = lax.ppermute(block, "mode", flip(n, 1))
    far = {b: lax.ppermute(block, "mode", flip(n, b)) for b in (2, 4, 6)}
    table = scatter_rows((0, 1), bases, idx, [block, near])
    for b in (2, 4, 6):
        other = lax.ppermute(far[b], "mode", flip(n, 1))
        table = scatter_rows((b, b ^ 1), bases, idx, [far[b], other], table)
    return table


def local(frames, phase_steps, pattern_rows, probes):
    columns = frames.shape[2]
    rows = frames.shape[1]
    groups = lax.axis_size("mode")
    pixels = rows * lax.axis_size("pix")
    modes_total = columns * groups
    k = probes.shape[1]
    vectors = 2 * k
    probes = probes.reshape(vectors, modes_total)
    here = jnp.stack([lax.axis_index("mode"), lax.axis_index("pix")]).astype(jnp.int32)
    steps_at = jnp.sum(
        jnp.where(phase_steps[None, :] == jnp.arange(4)[:, None], jnp.arange(4)[None, :], 0), axis=1
    ).astype(jnp.int32)
    my_rows = lax.dynamic_slice_in_dim(pattern_rows, lax.axis_index("mode") * columns, columns)
    scale = 1.0 / math.sqrt(modes_total)
    dh, dl, images, masks, bases = start(here, my_rows, steps_at, probes, frames, scale)
    odds = [masks[b : b + 1, :1] != 0 for b in range(8)]
    inv = inverse_factor(pack(gram(probes)), k)
    images, _ = sum_mode(images, odds)
    returned = sum_pix(backward(inv, images, dh, dl), odds)
    for iteration in range(1, ITERS):
        images, packed = forward(returned, dh, dl)
        images, packed = sum_mode(images, odds, packed)
        inv = inverse_factor(packed, k)
        returned = normalise(inv, sum_pix(backward(None, images, dh, dl), odds))
    table = gather_rows(returned, bases, pattern_rows)
    images, packed = forward(returned, dh, dl, groups)
    fields, packed = scatter_mode(images, odds, packed)
    inv = inverse_factor(packed, k)
    fields = normalise(inv, fields)
    power = jnp.sum(fields * fields, axis=1)
    power = jnp.broadcast_to((power[:k] + power[k:])[None, :], (8, k))
    power = double_sum(double_sum(power, "mode"), "pix")
    strengths = power[0] / pixels
    channels = end_vectors(inv, table, vectors)
    return (channels.reshape(2, k, modes_total), fields.reshape(2, k, -1), strengths)


def solution(mesh):
    in_specs = (P(None, "pix", "mode"), P(), P(), P())
    out_specs = (P(), P(None, None, ("pix", "mode")), P())
    return jax.shard_map(local, mesh=mesh, in_specs=in_specs, out_specs=out_specs, check_vma=False)
```

```python
import functools
import math

import jax
import jax.numpy as jnp
from jax import lax
from jax.experimental import pallas as pl
from jax.experimental.pallas import tpu as pltpu
from jax.sharding import PartitionSpec as P

HB = 128
ITERS = 2
BLOCK = 256
HW = 256
F32 = jnp.float32
BF16 = jnp.bfloat16

precise = lax.Precision.HIGHEST
NT = (((1,), (1,)), ((), ()))
NN = (((1,), (0,)), ((), ()))
VMEM = pl.BlockSpec(memory_space=pltpu.VMEM)
SMEM = pl.BlockSpec(memory_space=pltpu.SMEM)


def dot(a, b, dims):
    return lax.dot_general(a, b, dims, preferred_element_type=F32)


def exact(a, b, dims):
    return lax.dot_general(a, b, dims, precision=precise, preferred_element_type=F32)


def in_vmem(x):
    return pltpu.with_memory_space_constraint(x, pltpu.VMEM)


def split(values):
    high = values.astype(BF16)
    return high, (values - high.astype(F32)).astype(BF16)


def sign_table(order):
    row = lax.broadcasted_iota(jnp.int32, (order, order), 0)
    common = row & lax.broadcasted_iota(jnp.int32, (order, order), 1)
    parity = common
    shift = 16
    while shift:
        parity = parity ^ (parity >> shift)
        shift //= 2
    return (1 - 2 * (parity & 1)).astype(F32)


def butterfly(ref, count, width):
    rows = ref.shape[0]
    step = 1
    while step < count:
        radix = min(8, count // step)

        def body(g, carry, step=step, radix=radix):
            base = (g // step) * (step * radix) + g % step
            for s in range(rows // 8):
                for lane in range(0, width, HB):
                    at = [
                        pl.multiple_of((base + r * step) * width + lane, HB) for r in range(radix)
                    ]
                    v = [ref[s * 8 : s * 8 + 8, pl.ds(a, HB)] for a in at]
                    half = 1
                    while half < radix:
                        v = [
                            v[r] + v[r + half] if not r & half else v[r - half] - v[r]
                            for r in range(radix)
                        ]
                        half *= 2
                    for a, x in zip(at, v):
                        ref[s * 8 : s * 8 + 8, pl.ds(a, HB)] = x
            return carry

        lax.fori_loop(0, count // radix, body, 0)
        step *= radix


def block_loop(count, unroll, body):
    unroll = math.gcd(count, unroll)

    def many(i, carry):
        for q in range(unroll):
            body(i * unroll + q)
        return carry

    lax.fori_loop(0, count // unroll, many, 0)


def start_kernel(
    scale, steps_ref, idx_ref, probes_ref, frames_ref,
    dh_ref, dl_ref, img_ref, mask_ref, base_ref, f_ref, w_ref, n_ref, g_ref, b_ref, t_ref, sems, sem,
):
    vectors, modes = probes_ref.shape
    steps, rows, count = frames_ref.shape
    outer = modes // HW
    block = min(BLOCK, rows)
    first = pltpu.make_async_copy(probes_ref, w_ref, sem)
    first.start()
    copies = [
        [
            pltpu.make_async_copy(
                frames_ref.at[s, pl.ds(i * block, block)],
                f_ref.at[s, pl.ds(i * block, block)],
                sems.at[s, i],
            )
            for s in range(steps)
        ]
        for i in range(rows // block)
    ]
    for row in copies:
        for c in row:
            c.start()
    here = (lax.axis_index("mode"), lax.axis_index("pix"))
    for b in range(4):
        for place, axis_row in ((here[0], 0), (here[1], 4)):
            bit = ((place >> b) & 1).astype(F32)
            mask_ref[axis_row + b : axis_row + b + 1, :] = jnp.full((1, HB), bit, F32)
    for b in range(base_ref.shape[0]):
        base_ref[b] = (here[0] ^ b) * count
    signs = sign_table(HW).astype(BF16)
    first.wait()
    butterfly(w_ref, outer, HW)

    def inner(i):
        at = pl.multiple_of(i * HW, HW)
        both = jnp.concatenate(split(w_ref[:, pl.ds(at, HW)]), axis=0)
        n_ref[pl.ds(at, HW), :] = dot(signs, both, NT)

    block_loop(outer, 8, inner)
    start_at = here[0] * count

    def gather(t, carry):
        at = pl.multiple_of(t * 32, 32)
        for q in range(32):
            g_ref[pl.ds(at + q, 1), :] = n_ref[pl.ds(idx_ref[start_at + at + q], 1), :]
        return carry

    lax.fori_loop(0, count // 32, gather, 0)
    parts = [g_ref[b * HB : (b + 1) * HB, :].T for b in range(count // HB)]
    parts = [p[:vectors] + p[vectors:] for p in parts]
    b_ref[...], t_ref[...] = stack_forward(jnp.concatenate(parts, axis=1) * scale)
    frame = [
        sum(jnp.where(steps_ref[f] == s, f, 0) for f in range(1, steps)) for s in range(steps)
    ]
    for i, row in enumerate(copies):
        for c in row:
            c.wait()
        span = slice(i * block, (i + 1) * block)
        for part in (0, 1):
            high, low = split(0.25 * (f_ref[frame[part], span] - f_ref[frame[part + 2], span]))
            dh_ref[part, span] = high
            dl_ref[part, span] = low
        img_ref[:, span] = apply_forward(b_ref[...], t_ref[...], dh_ref, dl_ref, span)


def cost(us):
    return pl.CostEstimate(flops=0, transcendentals=0, bytes_accessed=int(us * 3.5e6))


def start(phase_steps, idx, probes, frames, scale):
    vectors, modes = probes.shape
    steps, rows, count = frames.shape
    planes = pltpu.VMEM((2, rows, count), BF16)
    hbm = pl.BlockSpec(memory_space=pltpu.HBM)
    return pl.pallas_call(
        functools.partial(start_kernel, scale),
        out_shape=[
            planes,
            planes,
            jax.ShapeDtypeStruct((vectors, rows), F32),
            jax.ShapeDtypeStruct((8, HB), F32),
            jax.ShapeDtypeStruct((modes // count,), jnp.int32),
        ],
        in_specs=[SMEM, SMEM, hbm, hbm],
        out_specs=[VMEM, VMEM, VMEM, VMEM, SMEM],
        cost_estimate=cost(12),
        scratch_shapes=[
            pltpu.VMEM((steps, rows, count), F32),
            pltpu.VMEM((vectors, modes), F32),
            pltpu.VMEM((modes, HB), F32),
            pltpu.VMEM((count, HB), F32),
            pltpu.VMEM((2 * vectors, count), BF16),
            pltpu.VMEM((2 * vectors, count), BF16),
            pltpu.SemaphoreType.DMA((steps, rows // min(BLOCK, rows))),
            pltpu.SemaphoreType.DMA,
        ],
        compiler_params=pltpu.CompilerParams(vmem_limit_bytes=44 << 20),
    )(phase_steps, idx, probes, frames)


def scatter_kernel(places, base_ref, idx_ref, *refs):
    s_ref, w_ref = refs[-1], refs[-2]
    pieces = [r for r in refs[:-2] if len(r.shape) == 2 and r.shape[1] == s_ref.shape[0]]
    count = s_ref.shape[0]
    for p, x_ref in enumerate(pieces):
        for i in range(count // HB):
            high, low = split(x_ref[:, i * HB : (i + 1) * HB])
            both = jnp.concatenate([high.astype(F32), low.astype(F32)], axis=0)
            s_ref[i * HB : (i + 1) * HB, :] = both.T
        base = base_ref[places[p]]

        def move(t, carry, base=base):
            at = pl.multiple_of(t * 32, 32)
            for q in range(32):
                w_ref[pl.ds(idx_ref[base + at + q], 1), :] = s_ref[pl.ds(at + q, 1), :]
            return carry

        lax.fori_loop(0, count // 32, move, 0)


def scatter_rows(places, bases, idx, pieces, table=None):
    count = pieces[0].shape[1]
    args = [bases, idx, *pieces] + ([] if table is None else [table])
    return pl.pallas_call(
        functools.partial(scatter_kernel, places),
        cost_estimate=cost(1.7 * len(pieces)),
        out_shape=jax.ShapeDtypeStruct((idx.shape[0], HB), F32),
        in_specs=[SMEM, SMEM] + [VMEM] * (len(args) - 2),
        out_specs=VMEM,
        scratch_shapes=[pltpu.VMEM((count, HB), F32)],
        input_output_aliases={} if table is None else {len(args) - 1: 0},
        compiler_params=pltpu.CompilerParams(vmem_limit_bytes=8 << 20),
    )(*args)


def end_kernel(inv_ref, w_ref, out_ref):
    vectors, modes = out_ref.shape
    half = vectors // 2
    outer = modes // HW
    signs = sign_table(HW).astype(BF16)
    zero = jnp.zeros((half, half), F32)
    wide = jnp.concatenate(
        [jnp.concatenate([inv_ref[...], zero], 1), jnp.concatenate([zero, inv_ref[...]], 1)], 0
    )
    high, low = split(wide)
    mix = jnp.concatenate(
        [jnp.concatenate([high, high], 1), jnp.concatenate([low, jnp.zeros_like(low)], 1)], 0
    )

    def first(i):
        at = pl.multiple_of(i * HW, HW)
        both = dot(mix, w_ref[pl.ds(at, HW), :].astype(BF16), NT)
        out_ref[:, pl.ds(at, HW)] = both[:vectors] + both[vectors:]

    block_loop(outer, 8, first)
    butterfly(out_ref, outer, HW)

    def inner(i):
        at = pl.multiple_of(i * HW, HW)
        both = dot(jnp.concatenate(split(out_ref[:, pl.ds(at, HW)]), axis=0), signs, NN)
        out_ref[:, pl.ds(at, HW)] = both[:vectors] + both[vectors:]

    block_loop(outer, 8, inner)


def end_vectors(inv, table, vectors):
    return pl.pallas_call(
        end_kernel,
        cost_estimate=cost(12),
        out_shape=jax.ShapeDtypeStruct((vectors, table.shape[0]), F32),
        in_specs=[VMEM, VMEM],
        out_specs=VMEM,
        compiler_params=pltpu.CompilerParams(vmem_limit_bytes=12 << 20),
    )(inv, table)


def factor_kernel(g_ref, out_ref):
    n = out_ref.shape[0]
    square = jnp.concatenate([g_ref[:, i * n : (i + 1) * n] for i in range(n // 8)], axis=0)
    row = lax.broadcasted_iota(jnp.int32, (n, n), 0)
    eye = (row == lax.broadcasted_iota(jnp.int32, (n, n), 1)).astype(F32)
    both = jnp.concatenate([square, eye], axis=1)
    below = lax.broadcasted_iota(jnp.int32, (n, 1), 0)
    for k in range(n - 1):
        scaled = both[k : k + 1] * (1.0 / both[k : k + 1, k : k + 1])
        both = both - jnp.where(below > k, both[:, k : k + 1], 0.0) * scaled
    pivots = jnp.sum(both[:, :n] * eye, axis=1, keepdims=True)
    out_ref[...] = both[:, n:] * (1.0 / jnp.sqrt(pivots))


def pack(gram_matrix):
    n = gram_matrix.shape[0]
    return jnp.concatenate([gram_matrix[i : i + 8] for i in range(0, n, 8)], axis=1)


def inverse_factor(packed, n):
    return pl.pallas_call(
        factor_kernel,
        cost_estimate=cost(2.7),
        out_shape=jax.ShapeDtypeStruct((n, n), F32),
        in_specs=[VMEM],
        out_specs=VMEM,
        compiler_params=pltpu.CompilerParams(vmem_limit_bytes=2 << 20),
    )(packed)


def stack_forward(u):
    half = u.shape[0] // 2
    turned = jnp.concatenate([-u[half:], u[:half]], axis=0)
    uh, ul = split(u)
    th, tl = split(turned)
    return jnp.concatenate([uh, ul], axis=0), jnp.concatenate([th, tl], axis=0)


def apply_forward(both, turned, dh, dl, span):
    n = both.shape[0] // 2
    wide = dot(both, dh[0, span], NT) + dot(turned, dh[1, span], NT)
    low = dot(both[:n], dl[0, span], NT) + dot(turned[:n], dl[1, span], NT)
    return wide[:n] + wide[n:] + low


def gram(vectors):
    half = vectors.shape[0] // 2
    return exact(vectors[:half], vectors[:half], NT) + exact(vectors[half:], vectors[half:], NT)


def forward_kernel(u_ref, dh_ref, dl_ref, img_ref, gram_ref):
    gram_ref[...] = pack(gram(u_ref[...]))
    both, turned = stack_forward(u_ref[...])
    rows = dh_ref.shape[1]
    block = min(BLOCK, rows)
    width = img_ref.shape[-1]
    for i in range(rows // block):
        part = apply_forward(both, turned, dh_ref, dl_ref, slice(i * block, (i + 1) * block))
        if len(img_ref.shape) == 2:
            img_ref[:, i * block : (i + 1) * block] = part
        else:
            for j in range(block // width):
                img_ref[i * block // width + j] = part[:, j * width : (j + 1) * width]


def forward(u, dh, dl, places=None):
    rows = dh.shape[1]
    vectors = u.shape[0]
    shape = (vectors, rows) if places is None else (places, vectors, rows // places)
    return pl.pallas_call(
        forward_kernel,
        out_shape=[
            jax.ShapeDtypeStruct(shape, F32),
            jax.ShapeDtypeStruct((8, vectors // 2 * vectors // 16), F32),
        ],
        in_specs=[VMEM, VMEM, VMEM],
        out_specs=[VMEM, VMEM],
        cost_estimate=cost(2.7),
        compiler_params=pltpu.CompilerParams(vmem_limit_bytes=12 << 20),
    )(u, in_vmem(dh), in_vmem(dl))


def backward_kernel(*refs):
    inv_ref = refs[0] if len(refs) == 5 else None
    img_ref, dh_ref, dl_ref, ret_ref = refs[-4:]
    vectors, _ = img_ref.shape
    half = vectors // 2
    real, imag = img_ref[:half], img_ref[half:]
    if inv_ref is not None:
        real = exact(inv_ref[...], real, NN)
        imag = exact(inv_ref[...], imag, NN)
    stacks = []
    for pair in ([real, imag], [imag, -real]):
        high, low = split(jnp.concatenate(pair, axis=0))
        stacks.append((high, jnp.concatenate([high, low], axis=0)))
    cols = dh_ref.shape[2]
    block = min(BLOCK, cols)
    for i in range(cols // block):
        span = slice(i * block, (i + 1) * block)
        wide = dot(stacks[0][1], dh_ref[0, :, span], NN) + dot(stacks[1][1], dh_ref[1, :, span], NN)
        low = dot(stacks[0][0], dl_ref[0, :, span], NN) + dot(stacks[1][0], dl_ref[1, :, span], NN)
        ret_ref[:, span] = wide[:vectors] + wide[vectors:] + low


def backward(inv, images, dh, dl):
    args = ([] if inv is None else [inv]) + [images, in_vmem(dh), in_vmem(dl)]
    return pl.pallas_call(
        backward_kernel,
        cost_estimate=cost(1.6),
        out_shape=jax.ShapeDtypeStruct((images.shape[0], dh.shape[2]), F32),
        in_specs=[VMEM] * len(args),
        out_specs=VMEM,
        compiler_params=pltpu.CompilerParams(vmem_limit_bytes=12 << 20),
    )(*args)


def normalise(inv, vectors):
    half = inv.shape[0]
    return jnp.concatenate([exact(inv, vectors[:half], NN), exact(inv, vectors[half:], NN)], axis=0)


def flip(n, bit):
    return [(i, i ^ bit) for i in range(n)]


def pick(pieces, odds):
    for bit, odd in enumerate(odds):
        pieces = [jnp.where(odd, pieces[b ^ (1 << bit)], pieces[b]) for b in range(len(pieces))]
    return pieces


def scatter_sum(blocks, axis, step, odds):
    size = lax.axis_size(axis)
    mine = pick(blocks, odds)
    total = mine[0]
    for b in range(len(blocks) - 1, 0, -1):
        total = total + lax.ppermute(mine[b], axis, flip(size, b * step))
    return total


def gather_all(block, axis, step, odds):
    size = lax.axis_size(axis)
    far = [block]
    for b in range(1, 2 ** len(odds)):
        far.append(lax.ppermute(block, axis, flip(size, b * step)))
    return pick(far, odds)


def share_sum(block, axis, step, n):
    size = lax.axis_size(axis)
    total = block
    for b in range(n - 1, 0, -1):
        total = total + lax.ppermute(block, axis, flip(size, b * step))
    return total


def double_sum(block, axis):
    size = lax.axis_size(axis)
    bit = 1
    while bit < size:
        block = block + lax.ppermute(block, axis, flip(size, bit))
        bit *= 2
    return block


def sum_pix(x, odds):
    n = lax.axis_size("pix")
    if n != 4:
        return double_sum(x, "pix")
    rows = x.shape[0] // n
    odds = odds[4:6]
    blocks = [x[i * rows : (i + 1) * rows] for i in range(n)]
    mine = scatter_sum(blocks, "pix", 1, odds)
    return jnp.concatenate(gather_all(mine, "pix", 1, odds), axis=0)


def sum_mode(x, odds, extra=None):
    n = lax.axis_size("mode")
    rows, cols = x.shape
    if n != 8:
        small = None if extra is None else double_sum(extra, "mode")
        return double_sum(x, "mode"), small
    half = rows // 2
    odd = odds[0]
    mine = jnp.where(odd, x[half:], x[:half])
    other = jnp.where(odd, x[:half], x[half:])
    if extra is not None:
        width = extra.shape[1]
        row = jnp.pad(extra, ((0, 0), (0, cols - width)))
        mine = jnp.concatenate([mine, row], axis=0)
        other = jnp.concatenate([other, row], axis=0)
    chip = mine + lax.ppermute(other, "mode", flip(n, 1))
    chip = share_sum(chip, "mode", 2, 4)
    mine = chip[:half]
    other = lax.ppermute(mine, "mode", flip(n, 1))
    total = jnp.concatenate([jnp.where(odd, other, mine), jnp.where(odd, mine, other)], axis=0)
    return total, (None if extra is None else chip[half:, :width])


def scatter_mode(pieces, odds, extra):
    _, rows, width = pieces.shape
    n = lax.axis_size("mode")
    here = lax.axis_index("mode")
    if n != 8:
        total = double_sum(pieces, "mode")
        return lax.dynamic_index_in_dim(total, here, 0, False), double_sum(extra, "mode")
    odd = odds[0]
    mine = jnp.concatenate([jnp.where(odd, pieces[2 * i + 1], pieces[2 * i]) for i in range(4)])
    other = [jnp.where(odd, pieces[2 * i], pieces[2 * i + 1]) for i in range(4)]
    small = jnp.pad(extra, ((0, 0), (0, width - extra.shape[1])))
    got = lax.ppermute(jnp.concatenate(other + [small], axis=0), "mode", flip(n, 1))
    mine = mine + got[: 4 * rows]
    small = small + got[4 * rows :]
    blocks = [
        jnp.concatenate([mine[i * rows : (i + 1) * rows], small], axis=0) for i in range(4)
    ]
    total = scatter_sum(blocks, "mode", 2, odds[1:3])
    return total[:rows], total[rows:, : extra.shape[1]]


def gather_rows(block, bases, idx):
    n = lax.axis_size("mode")
    if n != 8:
        pieces = [block]
        bit = 1
        while bit < n:
            pieces = pieces + [lax.ppermute(p, "mode", flip(n, bit)) for p in pieces]
            bit *= 2
        return scatter_rows(range(n), bases, idx, pieces)
    got = {}
    for b in (6, 4, 2, 1):
        got[b] = lax.ppermute(block, "mode", flip(n, b))
    table = scatter_rows((0, 1), bases, idx, [block, got[1]])
    for b in (2, 4, 6):
        other = lax.ppermute(got[b], "mode", flip(n, 1))
        table = scatter_rows((b, b ^ 1), bases, idx, [got[b], other], table)
    return table


def measure(frames, phase_steps, pattern_rows, probes):
    columns = frames.shape[2]
    rows = frames.shape[1]
    groups = lax.axis_size("mode")
    pixels = rows * lax.axis_size("pix")
    modes_total = columns * groups
    k = probes.shape[1]
    vectors = 2 * k
    probes = probes.reshape(vectors, modes_total)
    scale = 1.0 / math.sqrt(modes_total)
    dh, dl, images, masks, bases = start(phase_steps, pattern_rows, probes, frames, scale)
    odds = [masks[b : b + 1, :1] != 0 for b in range(8)]
    inv = inverse_factor(pack(gram(probes)), k)
    images, _ = sum_mode(images, odds)
    partial = backward(inv, images, dh, dl)
    returned = sum_pix(partial, odds)
    for _ in range(1, ITERS):
        images, packed = forward(returned, dh, dl)
        images, packed = sum_mode(images, odds, packed)
        inv = inverse_factor(packed, k)
        partial = backward(None, images, dh, dl)
        returned = normalise(inv, sum_pix(partial, odds))
    table = gather_rows(returned, bases, pattern_rows)
    images, packed = forward(returned, dh, dl, groups)
    fields, packed = scatter_mode(images, odds, packed)
    inv = inverse_factor(packed, k)
    fields = normalise(inv, fields)
    power = jnp.sum(fields * fields, axis=1)
    power = jnp.broadcast_to((power[:k] + power[k:])[None, :], (8, k))
    power = double_sum(double_sum(power, "mode"), "pix")
    strengths = power[0] / pixels
    channels = end_vectors(inv, table, vectors)
    return (channels.reshape(2, k, modes_total), fields.reshape(2, k, -1), strengths)


def solution(mesh):
    in_specs = (P(None, "pix", "mode"), P(), P(), P())
    out_specs = (P(), P(None, None, ("pix", "mode")), P())
    return jax.shard_map(
        measure, mesh=mesh, in_specs=in_specs, out_specs=out_specs, check_vma=False
    )
```

```python
import functools
import math

import jax
import jax.numpy as jnp
from jax import lax
from jax.experimental import pallas as pl
from jax.experimental.pallas import tpu as pltpu
from jax.sharding import PartitionSpec as P

HB = 128
ITERS = 2
BLOCK = 256
HW = 256
COPY = 512
F32 = jnp.float32
BF16 = jnp.bfloat16

precise = lax.Precision.HIGHEST
NT = (((1,), (1,)), ((), ()))
NN = (((1,), (0,)), ((), ()))
VMEM = pl.BlockSpec(memory_space=pltpu.VMEM)
SMEM = pl.BlockSpec(memory_space=pltpu.SMEM)


def dot(a, b, dims):
    return lax.dot_general(a, b, dims, preferred_element_type=F32)


def exact(a, b, dims):
    return lax.dot_general(a, b, dims, precision=precise, preferred_element_type=F32)


def in_vmem(x):
    return pltpu.with_memory_space_constraint(x, pltpu.VMEM)


def split(values):
    high = values.astype(BF16)
    return high, (values - high.astype(F32)).astype(BF16)


def sign_table(order):
    row = lax.broadcasted_iota(jnp.int32, (order, order), 0)
    common = row & lax.broadcasted_iota(jnp.int32, (order, order), 1)
    parity = common
    shift = 16
    while shift:
        parity = parity ^ (parity >> shift)
        shift //= 2
    return (1 - 2 * (parity & 1)).astype(F32)


def butterfly(src, dst, count, width):
    rows = src.shape[0]
    step = 1
    while step < count:
        radix = min(32, count // step)
        for g in range(count // radix):
            base = (g // step) * (step * radix) + g % step
            for s in range(0, rows, 8):
                for lane in range(0, width, HB):
                    at = [(base + r * step) * width + lane for r in range(radix)]
                    v = [src[s : s + 8, a : a + HB] for a in at]
                    half = 1
                    while half < radix:
                        v = [
                            v[r] + v[r + half] if not r & half else v[r - half] - v[r]
                            for r in range(radix)
                        ]
                        half *= 2
                    for a, x in zip(at, v):
                        dst[s : s + 8, a : a + HB] = x
        step *= radix
        src = dst


def block_loop(count, unroll, body):
    unroll = math.gcd(count, unroll)

    def many(i, carry):
        for q in range(unroll):
            body(i * unroll + q)
        return carry

    lax.fori_loop(0, count // unroll, many, 0)


def start_kernel(
    scale, phase_ref, rows_ref, probes_ref, frames_ref,
    dh_ref, dl_ref, img_ref, mask_ref, base_ref, f_ref, p_ref, w_ref, n_ref, g_ref, b_ref, t_ref, idx_ref, steps_ref,
    sems, sem, tiny,
):
    vectors, modes = probes_ref.shape
    steps, rows, count = frames_ref.shape
    outer = modes // HW
    block = min(COPY, rows)
    small = [
        pltpu.make_async_copy(rows_ref, idx_ref, tiny.at[0]),
        pltpu.make_async_copy(phase_ref, steps_ref, tiny.at[1]),
    ]
    for c in small:
        c.start()
    first = pltpu.make_async_copy(probes_ref, p_ref, sem)
    first.start()
    copies = [
        [
            pltpu.make_async_copy(
                frames_ref.at[s, pl.ds(i * block, block)],
                f_ref.at[s, pl.ds(i * block, block)],
                sems.at[s, i],
            )
            for s in range(steps)
        ]
        for i in range(rows // block)
    ]
    here = (lax.axis_index("mode"), lax.axis_index("pix"))
    for b in range(4):
        for place, axis_row in ((here[0], 0), (here[1], 4)):
            bit = ((place >> b) & 1).astype(F32)
            mask_ref[axis_row + b : axis_row + b + 1, :] = jnp.full((1, HB), bit, F32)
    for b in range(base_ref.shape[0]):
        base_ref[b] = (here[0] ^ b) * count
    signs = sign_table(HW).astype(BF16)
    first.wait()
    half = (len(copies) + 1) // 2
    for row in copies[:half]:
        for c in row:
            c.start()
    butterfly(p_ref, w_ref, outer, HW)

    def inner(i):
        at = pl.multiple_of(i * HW, HW)
        both = jnp.concatenate(split(w_ref[:, pl.ds(at, HW)]), axis=0)
        n_ref[pl.ds(at, HW), :] = dot(signs, both, NT)

    block_loop(outer, 8, inner)
    for row in copies[half:]:
        for c in row:
            c.start()
    start_at = here[0] * count
    small[0].wait()

    def gather(t, carry):
        at = pl.multiple_of(t * 32, 32)
        for q in range(32):
            g_ref[pl.ds(at + q, 1), :] = n_ref[pl.ds(idx_ref[start_at + at + q], 1), :]
        return carry

    lax.fori_loop(0, count // 32, gather, 0)
    parts = [g_ref[b * HB : (b + 1) * HB, :].T for b in range(count // HB)]
    parts = [p[:vectors] + p[vectors:] for p in parts]
    b_ref[...], t_ref[...] = stack_forward(jnp.concatenate(parts, axis=1) * scale)
    small[1].wait()
    frame = [
        sum(jnp.where(steps_ref[f] == s, f, 0) for f in range(1, steps)) for s in range(steps)
    ]
    for i, row in enumerate(copies):
        for c in row:
            c.wait()
        span = slice(i * block, (i + 1) * block)
        for part in (0, 1):
            high, low = split(0.25 * (f_ref[frame[part], span] - f_ref[frame[part + 2], span]))
            dh_ref[part, span] = high
            dl_ref[part, span] = low
        img_ref[:, span] = apply_forward(b_ref[...], t_ref[...], dh_ref, dl_ref, span)


def cost(us):
    return pl.CostEstimate(flops=0, transcendentals=0, bytes_accessed=int(us * 3.5e6))


def start(phase_steps, idx, probes, frames, scale):
    vectors, modes = probes.shape
    steps, rows, count = frames.shape
    planes = pltpu.VMEM((2, rows, count), BF16)
    hbm = pl.BlockSpec(memory_space=pltpu.HBM)
    return pl.pallas_call(
        functools.partial(start_kernel, scale),
        out_shape=[
            planes,
            planes,
            jax.ShapeDtypeStruct((vectors, rows), F32),
            jax.ShapeDtypeStruct((8, HB), F32),
            jax.ShapeDtypeStruct((modes // count,), jnp.int32),
        ],
        in_specs=[hbm, hbm, hbm, hbm],
        out_specs=[VMEM, VMEM, VMEM, VMEM, SMEM],
        cost_estimate=cost(12),
        scratch_shapes=[
            pltpu.VMEM((steps, rows, count), F32),
            pltpu.VMEM((vectors, modes), F32),
            pltpu.VMEM((vectors, modes), F32),
            pltpu.VMEM((modes, HB), F32),
            pltpu.VMEM((count, HB), F32),
            pltpu.VMEM((2 * vectors, count), BF16),
            pltpu.VMEM((2 * vectors, count), BF16),
            pltpu.SMEM((modes,), jnp.int32),
            pltpu.SMEM((steps,), jnp.int32),
            pltpu.SemaphoreType.DMA((steps, rows // min(COPY, rows))),
            pltpu.SemaphoreType.DMA,
            pltpu.SemaphoreType.DMA((2,)),
        ],
        compiler_params=pltpu.CompilerParams(vmem_limit_bytes=44 << 20),
    )(*[pltpu.with_memory_space_constraint(x, pltpu.HBM) for x in (phase_steps, idx, probes, frames)])


def scatter_kernel(places, base_ref, idx_ref, *refs):
    s_ref, w_ref = refs[-1], refs[-2]
    pieces = [r for r in refs[:-2] if len(r.shape) == 2 and r.shape[1] == s_ref.shape[0]]
    count = s_ref.shape[0]
    for p, x_ref in enumerate(pieces):
        for i in range(count // HB):
            high, low = split(x_ref[:, i * HB : (i + 1) * HB])
            both = jnp.concatenate([high.astype(F32), low.astype(F32)], axis=0)
            s_ref[i * HB : (i + 1) * HB, :] = both.T
        base = base_ref[places[p]]

        def move(t, carry, base=base):
            at = pl.multiple_of(t * 32, 32)
            for q in range(32):
                w_ref[pl.ds(idx_ref[base + at + q], 1), :] = s_ref[pl.ds(at + q, 1), :]
            return carry

        lax.fori_loop(0, count // 32, move, 0)


def scatter_rows(places, bases, idx, pieces, table=None):
    count = pieces[0].shape[1]
    args = [bases, idx, *pieces] + ([] if table is None else [table])
    return pl.pallas_call(
        functools.partial(scatter_kernel, places),
        cost_estimate=cost(1.7 * len(pieces)),
        out_shape=jax.ShapeDtypeStruct((idx.shape[0], HB), F32),
        in_specs=[SMEM, SMEM] + [VMEM] * (len(args) - 2),
        out_specs=VMEM,
        scratch_shapes=[pltpu.VMEM((count, HB), F32)],
        input_output_aliases={} if table is None else {len(args) - 1: 0},
        compiler_params=pltpu.CompilerParams(vmem_limit_bytes=8 << 20),
    )(*args)


def end_kernel(inv_ref, w_ref, out_ref, y_ref, z_ref, o_ref, sems):
    vectors, modes = out_ref.shape
    half = vectors // 2
    outer = modes // HW
    signs = sign_table(HW).astype(BF16)
    zero = jnp.zeros((half, half), F32)
    wide = jnp.concatenate(
        [jnp.concatenate([inv_ref[...], zero], 1), jnp.concatenate([zero, inv_ref[...]], 1)], 0
    )
    high, low = split(wide)
    mix = jnp.concatenate(
        [jnp.concatenate([high, high], 1), jnp.concatenate([low, jnp.zeros_like(low)], 1)], 0
    )

    def first(i):
        at = pl.multiple_of(i * HW, HW)
        both = dot(mix, w_ref[pl.ds(at, HW), :].astype(BF16), NT)
        y_ref[:, pl.ds(at, HW)] = both[:vectors] + both[vectors:]

    block_loop(outer, 8, first)
    butterfly(y_ref, z_ref, outer, HW)
    per = modes // sems.shape[0]
    copies = [
        pltpu.make_async_copy(
            o_ref.at[:, pl.ds(c * per, per)], out_ref.at[:, pl.ds(c * per, per)], sems.at[c]
        )
        for c in range(sems.shape[0])
    ]
    for c, copy in enumerate(copies):
        for i in range(c * per, (c + 1) * per, HW):
            both = dot(jnp.concatenate(split(z_ref[:, i : i + HW]), axis=0), signs, NN)
            o_ref[:, i : i + HW] = both[:vectors] + both[vectors:]
        copy.start()
    for copy in copies:
        copy.wait()


def end_vectors(inv, table, vectors):
    return pl.pallas_call(
        end_kernel,
        cost_estimate=cost(6),
        out_shape=jax.ShapeDtypeStruct((vectors, table.shape[0]), F32),
        in_specs=[VMEM, VMEM],
        out_specs=pl.BlockSpec(memory_space=pltpu.HBM),
        scratch_shapes=[pltpu.VMEM((vectors, table.shape[0]), F32)] * 3
        + [pltpu.SemaphoreType.DMA((4,))],
        compiler_params=pltpu.CompilerParams(vmem_limit_bytes=14 << 20),
    )(inv, table)


def factor_kernel(g_ref, out_ref):
    n = out_ref.shape[0]
    square = jnp.concatenate([g_ref[:, i * n : (i + 1) * n] for i in range(n // 8)], axis=0)
    row = lax.broadcasted_iota(jnp.int32, (n, n), 0)
    eye = (row == lax.broadcasted_iota(jnp.int32, (n, n), 1)).astype(F32)
    both = jnp.concatenate([square, eye], axis=1)
    below = lax.broadcasted_iota(jnp.int32, (n, 1), 0)
    for k in range(n - 1):
        scaled = both[k : k + 1] * (1.0 / both[k : k + 1, k : k + 1])
        both = both - jnp.where(below > k, both[:, k : k + 1], 0.0) * scaled
    pivots = jnp.sum(both[:, :n] * eye, axis=1, keepdims=True)
    out_ref[...] = both[:, n:] * (1.0 / jnp.sqrt(pivots))


def pack(gram_matrix):
    n = gram_matrix.shape[0]
    return jnp.concatenate([gram_matrix[i : i + 8] for i in range(0, n, 8)], axis=1)


def inverse_factor(packed, n):
    return pl.pallas_call(
        factor_kernel,
        cost_estimate=cost(2.7),
        out_shape=jax.ShapeDtypeStruct((n, n), F32),
        in_specs=[VMEM],
        out_specs=VMEM,
        compiler_params=pltpu.CompilerParams(vmem_limit_bytes=2 << 20),
    )(packed)


def stack_forward(u):
    half = u.shape[0] // 2
    turned = jnp.concatenate([-u[half:], u[:half]], axis=0)
    uh, ul = split(u)
    th, tl = split(turned)
    return jnp.concatenate([uh, ul], axis=0), jnp.concatenate([th, tl], axis=0)


def apply_forward(both, turned, dh, dl, span):
    n = both.shape[0] // 2
    wide = dot(both, dh[0, span], NT) + dot(turned, dh[1, span], NT)
    low = dot(both[:n], dl[0, span], NT) + dot(turned[:n], dl[1, span], NT)
    return wide[:n] + wide[n:] + low


def gram(vectors):
    half = vectors.shape[0] // 2
    return exact(vectors[:half], vectors[:half], NT) + exact(vectors[half:], vectors[half:], NT)


def forward_kernel(u_ref, dh_ref, dl_ref, img_ref, gram_ref):
    gram_ref[...] = pack(gram(u_ref[...]))
    both, turned = stack_forward(u_ref[...])
    rows = dh_ref.shape[1]
    block = min(BLOCK, rows)
    width = img_ref.shape[-1]
    for i in range(rows // block):
        part = apply_forward(both, turned, dh_ref, dl_ref, slice(i * block, (i + 1) * block))
        if len(img_ref.shape) == 2:
            img_ref[:, i * block : (i + 1) * block] = part
        else:
            for j in range(block // width):
                img_ref[i * block // width + j] = part[:, j * width : (j + 1) * width]


def forward(u, dh, dl, places=None):
    rows = dh.shape[1]
    vectors = u.shape[0]
    shape = (vectors, rows) if places is None else (places, vectors, rows // places)
    return pl.pallas_call(
        forward_kernel,
        out_shape=[
            jax.ShapeDtypeStruct(shape, F32),
            jax.ShapeDtypeStruct((8, vectors // 2 * vectors // 16), F32),
        ],
        in_specs=[VMEM, VMEM, VMEM],
        out_specs=[VMEM, VMEM],
        cost_estimate=cost(2.7),
        compiler_params=pltpu.CompilerParams(vmem_limit_bytes=12 << 20),
    )(u, in_vmem(dh), in_vmem(dl))


def backward_kernel(*refs):
    inv_ref = refs[0] if len(refs) == 5 else None
    img_ref, dh_ref, dl_ref, ret_ref = refs[-4:]
    vectors, _ = img_ref.shape
    half = vectors // 2
    real, imag = img_ref[:half], img_ref[half:]
    if inv_ref is not None:
        real = exact(inv_ref[...], real, NN)
        imag = exact(inv_ref[...], imag, NN)
    stacks = []
    for pair in ([real, imag], [imag, -real]):
        high, low = split(jnp.concatenate(pair, axis=0))
        stacks.append((high, jnp.concatenate([high, low], axis=0)))
    cols = dh_ref.shape[2]
    block = min(BLOCK, cols)
    for i in range(cols // block):
        span = slice(i * block, (i + 1) * block)
        wide = dot(stacks[0][1], dh_ref[0, :, span], NN) + dot(stacks[1][1], dh_ref[1, :, span], NN)
        low = dot(stacks[0][0], dl_ref[0, :, span], NN) + dot(stacks[1][0], dl_ref[1, :, span], NN)
        ret_ref[:, span] = wide[:vectors] + wide[vectors:] + low


def backward(inv, images, dh, dl):
    args = ([] if inv is None else [inv]) + [images, in_vmem(dh), in_vmem(dl)]
    return pl.pallas_call(
        backward_kernel,
        cost_estimate=cost(1.6),
        out_shape=jax.ShapeDtypeStruct((images.shape[0], dh.shape[2]), F32),
        in_specs=[VMEM] * len(args),
        out_specs=VMEM,
        compiler_params=pltpu.CompilerParams(vmem_limit_bytes=12 << 20),
    )(*args)


def normalise(inv, vectors):
    half = inv.shape[0]
    return jnp.concatenate([exact(inv, vectors[:half], NN), exact(inv, vectors[half:], NN)], axis=0)


def flip(n, bit):
    return [(i, i ^ bit) for i in range(n)]


def pick(pieces, odds):
    for bit, odd in enumerate(odds):
        pieces = [jnp.where(odd, pieces[b ^ (1 << bit)], pieces[b]) for b in range(len(pieces))]
    return pieces


def scatter_sum(blocks, axis, step, odds):
    size = lax.axis_size(axis)
    mine = pick(blocks, odds)
    total = mine[0]
    for b in range(len(blocks) - 1, 0, -1):
        total = total + lax.ppermute(mine[b], axis, flip(size, b * step))
    return total


def gather_all(block, axis, step, odds):
    size = lax.axis_size(axis)
    far = [block]
    for b in range(1, 2 ** len(odds)):
        far.append(lax.ppermute(block, axis, flip(size, b * step)))
    return pick(far, odds)


def share_sum(block, axis, step, n):
    size = lax.axis_size(axis)
    total = block
    for b in range(n - 1, 0, -1):
        total = total + lax.ppermute(block, axis, flip(size, b * step))
    return total


def double_sum(block, axis):
    size = lax.axis_size(axis)
    bit = 1
    while bit < size:
        block = block + lax.ppermute(block, axis, flip(size, bit))
        bit *= 2
    return block


def sum_pix(x, odds):
    n = lax.axis_size("pix")
    if n != 4:
        return double_sum(x, "pix")
    rows = x.shape[0] // n
    odds = odds[4:6]
    blocks = [x[i * rows : (i + 1) * rows] for i in range(n)]
    mine = scatter_sum(blocks, "pix", 1, odds)
    return jnp.concatenate(gather_all(mine, "pix", 1, odds), axis=0)


def sum_mode(x, odds, extra=None):
    n = lax.axis_size("mode")
    rows, cols = x.shape
    if n != 8:
        small = None if extra is None else double_sum(extra, "mode")
        return double_sum(x, "mode"), small
    half = rows // 2
    odd = odds[0]
    mine = jnp.where(odd, x[half:], x[:half])
    other = jnp.where(odd, x[:half], x[half:])
    if extra is not None:
        width = extra.shape[1]
        row = jnp.pad(extra, ((0, 0), (0, cols - width)))
        mine = jnp.concatenate([mine, row], axis=0)
        other = jnp.concatenate([other, row], axis=0)
    chip = mine + lax.ppermute(other, "mode", flip(n, 1))
    chip = share_sum(chip, "mode", 2, 4)
    mine = chip[:half]
    other = lax.ppermute(mine, "mode", flip(n, 1))
    total = jnp.concatenate([jnp.where(odd, other, mine), jnp.where(odd, mine, other)], axis=0)
    return total, (None if extra is None else chip[half:, :width])


def scatter_mode(pieces, odds, extra):
    _, rows, width = pieces.shape
    n = lax.axis_size("mode")
    here = lax.axis_index("mode")
    if n != 8:
        total = double_sum(pieces, "mode")
        return lax.dynamic_index_in_dim(total, here, 0, False), double_sum(extra, "mode")
    odd = odds[0]
    mine = jnp.concatenate([jnp.where(odd, pieces[2 * i + 1], pieces[2 * i]) for i in range(4)])
    other = [jnp.where(odd, pieces[2 * i], pieces[2 * i + 1]) for i in range(4)]
    small = jnp.pad(extra, ((0, 0), (0, width - extra.shape[1])))
    got = lax.ppermute(jnp.concatenate(other + [small], axis=0), "mode", flip(n, 1))
    mine = mine + got[: 4 * rows]
    small = small + got[4 * rows :]
    blocks = [
        jnp.concatenate([mine[i * rows : (i + 1) * rows], small], axis=0) for i in range(4)
    ]
    total = scatter_sum(blocks, "mode", 2, odds[1:3])
    return total[:rows], total[rows:, : extra.shape[1]]


def gather_rows(block, bases, idx):
    n = lax.axis_size("mode")
    if n != 8:
        pieces = [block]
        bit = 1
        while bit < n:
            pieces = pieces + [lax.ppermute(p, "mode", flip(n, bit)) for p in pieces]
            bit *= 2
        return scatter_rows(range(n), bases, idx, pieces)
    got = {}
    for b in (6, 4, 2, 1):
        got[b] = lax.ppermute(block, "mode", flip(n, b))
    table = scatter_rows((0, 1), bases, idx, [block, got[1]])
    for b in (2, 4, 6):
        other = lax.ppermute(got[b], "mode", flip(n, 1))
        table = scatter_rows((b, b ^ 1), bases, idx, [got[b], other], table)
    return table


def measure(frames, phase_steps, pattern_rows, probes):
    columns = frames.shape[2]
    rows = frames.shape[1]
    groups = lax.axis_size("mode")
    pixels = rows * lax.axis_size("pix")
    modes_total = columns * groups
    k = probes.shape[1]
    vectors = 2 * k
    probes = probes.reshape(vectors, modes_total)
    scale = 1.0 / math.sqrt(modes_total)
    dh, dl, images, masks, bases = start(phase_steps, pattern_rows, probes, frames, scale)
    odds = [masks[b : b + 1, :1] != 0 for b in range(8)]
    inv = inverse_factor(pack(gram(probes)), k)
    images, _ = sum_mode(images, odds)
    partial = backward(inv, images, dh, dl)
    returned = sum_pix(partial, odds)
    for _ in range(1, ITERS):
        images, packed = forward(returned, dh, dl)
        images, packed = sum_mode(images, odds, packed)
        inv = inverse_factor(packed, k)
        partial = backward(None, images, dh, dl)
        returned = normalise(inv, sum_pix(partial, odds))
    table = gather_rows(returned, bases, pattern_rows)
    images, packed = forward(returned, dh, dl, groups)
    fields, packed = scatter_mode(images, odds, packed)
    inv = inverse_factor(packed, k)
    fields = normalise(inv, fields)
    power = jnp.sum(fields * fields, axis=1)
    power = jnp.broadcast_to((power[:k] + power[k:])[None, :], (8, k))
    power = double_sum(double_sum(power, "mode"), "pix")
    strengths = power[0] / pixels
    channels = end_vectors(inv, table, vectors)
    return (channels.reshape(2, k, modes_total), fields.reshape(2, k, -1), strengths)


def solution(mesh):
    in_specs = (P(None, "pix", "mode"), P(), P(), P())
    out_specs = (P(), P(None, None, ("pix", "mode")), P())
    return jax.shard_map(
        measure, mesh=mesh, in_specs=in_specs, out_specs=out_specs, check_vma=False
    )
```

```python
import functools
import math

import jax
import jax.numpy as jnp
from jax import lax
from jax.experimental import pallas as pl
from jax.experimental.pallas import tpu as pltpu
from jax.sharding import PartitionSpec as P

HB = 128
ITERS = 2
BLOCK = 256
HW = 256
COPY = 512
F32 = jnp.float32
BF16 = jnp.bfloat16

precise = lax.Precision.HIGHEST
NT = (((1,), (1,)), ((), ()))
NN = (((1,), (0,)), ((), ()))
VMEM = pl.BlockSpec(memory_space=pltpu.VMEM)
SMEM = pl.BlockSpec(memory_space=pltpu.SMEM)


def dot(a, b, dims):
    return lax.dot_general(a, b, dims, preferred_element_type=F32)


def exact(a, b, dims):
    return lax.dot_general(a, b, dims, precision=precise, preferred_element_type=F32)


def in_vmem(x):
    return pltpu.with_memory_space_constraint(x, pltpu.VMEM)


def split(values):
    high = values.astype(BF16)
    return high, (values - high.astype(F32)).astype(BF16)


def sign_table(order):
    row = lax.broadcasted_iota(jnp.int32, (order, order), 0)
    common = row & lax.broadcasted_iota(jnp.int32, (order, order), 1)
    parity = common
    shift = 16
    while shift:
        parity = parity ^ (parity >> shift)
        shift //= 2
    return (1 - 2 * (parity & 1)).astype(F32)


def butterfly(src, dst, count, width):
    rows = src.shape[0]
    step = 1
    while step < count:
        radix = min(32, count // step)
        for g in range(count // radix):
            base = (g // step) * (step * radix) + g % step
            for s in range(0, rows, 8):
                for lane in range(0, width, HB):
                    at = [(base + r * step) * width + lane for r in range(radix)]
                    v = [src[s : s + 8, a : a + HB] for a in at]
                    half = 1
                    while half < radix:
                        v = [
                            v[r] + v[r + half] if not r & half else v[r - half] - v[r]
                            for r in range(radix)
                        ]
                        half *= 2
                    for a, x in zip(at, v):
                        dst[s : s + 8, a : a + HB] = x
        step *= radix
        src = dst


def block_loop(count, unroll, body):
    unroll = math.gcd(count, unroll)

    def many(i, carry):
        for q in range(unroll):
            body(i * unroll + q)
        return carry

    lax.fori_loop(0, count // unroll, many, 0)


def start_kernel(
    scale, cut, phase_ref, rows_ref, probes_ref, frames_ref,
    dh_ref, dl_ref, img_ref, mask_ref, base_ref, b_ref, t_ref, f_ref, p_ref, w_ref, n_ref, g_ref,
    idx_ref, steps_ref,
    sems, sem, tiny,
):
    vectors, modes = probes_ref.shape
    steps, rows, count = frames_ref.shape
    outer = modes // HW
    block = min(COPY, rows)
    small = [
        pltpu.make_async_copy(rows_ref, idx_ref, tiny.at[0]),
        pltpu.make_async_copy(phase_ref, steps_ref, tiny.at[1]),
    ]
    for c in small:
        c.start()
    first = pltpu.make_async_copy(probes_ref, p_ref, sem)
    first.start()
    copies = [
        [
            pltpu.make_async_copy(
                frames_ref.at[s, pl.ds(i * block, block)],
                f_ref.at[s, pl.ds(i * block, block)],
                sems.at[s, i],
            )
            for s in range(steps)
        ]
        for i in range(rows // block)
    ]
    here = (lax.axis_index("mode"), lax.axis_index("pix"))
    for b in range(4):
        for place, axis_row in ((here[0], 0), (here[1], 4)):
            bit = ((place >> b) & 1).astype(F32)
            mask_ref[axis_row + b : axis_row + b + 1, :] = jnp.full((1, HB), bit, F32)
    for b in range(base_ref.shape[0]):
        base_ref[b] = (here[0] ^ b) * count
    signs = sign_table(HW).astype(BF16)
    first.wait()
    half = (len(copies) + 1) // 2
    for row in copies[:half]:
        for c in row:
            c.start()
    butterfly(p_ref, w_ref, outer, HW)

    def inner(i):
        at = pl.multiple_of(i * HW, HW)
        both = jnp.concatenate(split(w_ref[:, pl.ds(at, HW)]), axis=0)
        n_ref[pl.ds(at, HW), :] = dot(signs, both, NT)

    block_loop(outer, 8, inner)
    for row in copies[half:]:
        for c in row:
            c.start()
    start_at = here[0] * count
    small[0].wait()

    def gather(t, carry):
        at = pl.multiple_of(t * 32, 32)
        for q in range(32):
            g_ref[pl.ds(at + q, 1), :] = n_ref[pl.ds(idx_ref[start_at + at + q], 1), :]
        return carry

    lax.fori_loop(0, count // 32, gather, 0)
    parts = [g_ref[b * HB : (b + 1) * HB, :].T for b in range(count // HB)]
    parts = [p[:vectors] + p[vectors:] for p in parts]
    b_ref[...], t_ref[...] = stack_forward(jnp.concatenate(parts, axis=1) * scale)
    small[1].wait()
    frame = [
        sum(jnp.where(steps_ref[f] == s, f, 0) for f in range(1, steps)) for s in range(steps)
    ]
    for i, row in enumerate(copies):
        for c in row:
            c.wait()
        span = slice(i * block, (i + 1) * block)
        for part in (0, 1):
            high, low = split(0.25 * (f_ref[frame[part], span] - f_ref[frame[part + 2], span]))
            dh_ref[part, span] = high
            dl_ref[part, span] = low
        if not cut:
            img_ref[:, span] = apply_forward(b_ref[...], t_ref[...], dh_ref, dl_ref, span)
    if cut:
        from_rows(img_ref, "other", b_ref[...], t_ref[...], dh_ref, dl_ref)


def side_start(side, rows):
    core = lax.axis_index("mode") & 1
    return pl.multiple_of((core if side == "own" else 1 - core) * (rows // 2), rows // 2)


def from_rows(img_ref, side, both, turned, dh_ref, dl_ref):
    rows = dh_ref.shape[1]
    base = side_start(side, rows)
    for i in range(0, rows // 2, BLOCK):
        span = pl.ds(base + i, BLOCK)
        img_ref[:, i : i + BLOCK] = apply_forward(both, turned, dh_ref, dl_ref, span)


def own_kernel(b_ref, t_ref, dh_ref, dl_ref, img_ref):
    from_rows(img_ref, "own", b_ref[...], t_ref[...], dh_ref, dl_ref)


def own_half(both, turned, dh, dl):
    return pl.pallas_call(
        own_kernel,
        out_shape=jax.ShapeDtypeStruct((both.shape[0] // 2, dh.shape[1] // 2), F32),
        in_specs=[VMEM] * 4,
        out_specs=VMEM,
        cost_estimate=cost(1.3),
        compiler_params=pltpu.CompilerParams(vmem_limit_bytes=8 << 20),
    )(both, turned, in_vmem(dh), in_vmem(dl))


def ahead_kernel(bits, side, has_inv, has_acc, places, *refs):
    refs = list(refs)
    inv = refs.pop(0)[...] if has_inv else None
    acc_ref, acc_gram = (refs.pop(0), refs.pop(0)) if has_acc else (None, None)
    pieces = [refs.pop(0)[...] for _ in bits]
    dh_ref, dl_ref, img_ref = refs[:3]
    here = lax.axis_index("pix")
    width = pieces[0].shape[1]
    half = pieces[0].shape[0] // 2
    if has_inv:
        pieces = [
            jnp.concatenate([exact(inv, p[:half], NN), exact(inv, p[half:], NN)], axis=0)
            for p in pieces
        ]
    if len(refs) > 3:
        total = pack(sum(gram(p) for p in pieces))
        refs[3][...] = total if acc_gram is None else total + acc_gram[...]
    stacks = [stack_forward(p) for p in pieces]
    cols = [pl.ds(pl.multiple_of((here ^ b) * width, width), width) for b in bits]
    rows = dh_ref.shape[1]
    base = 0 if side is None else side_start(side, rows)
    for i in range(0, rows if side is None else rows // 2, BLOCK):
        span = pl.ds(base + i, BLOCK)
        part = sum(apply_ahead(*st, dh_ref, dl_ref, span, col) for st, col in zip(stacks, cols))
        if acc_ref is not None:
            part = part + acc_ref[:, span]
        if places is None:
            img_ref[:, i : i + BLOCK] = part
        else:
            w = rows // places
            for j in range(BLOCK // w):
                img_ref[i // w + j] = part[:, j * w : (j + 1) * w]


def apply_ahead(both, turned, dh, dl, span, col):
    n = both.shape[0] // 2
    wide = dot(both, dh[0, span, col], NT) + dot(turned, dh[1, span, col], NT)
    low = dot(both[:n], dl[0, span, col], NT) + dot(turned[:n], dl[1, span, col], NT)
    return wide[:n] + wide[n:] + low


def ahead(pieces, bits, dh, dl, side=None, inv=None, acc=None, places=None, with_gram=True):
    rows = dh.shape[1]
    vectors = pieces[0].shape[0]
    shape = (vectors, rows if side is None else rows // 2)
    if places is not None:
        shape = (places, vectors, rows // places)
    out = [jax.ShapeDtypeStruct(shape, F32)]
    if with_gram:
        out.append(jax.ShapeDtypeStruct((8, vectors // 2 * vectors // 16), F32))
    args = ([] if inv is None else [inv]) + (list(acc) if acc else []) + list(pieces)
    args += [in_vmem(dh), in_vmem(dl)]
    kernel = functools.partial(
        ahead_kernel, tuple(bits), side, inv is not None, acc is not None, places
    )
    return pl.pallas_call(
        kernel,
        out_shape=out,
        in_specs=[VMEM] * len(args),
        out_specs=[VMEM] * len(out),
        cost_estimate=cost(0.7 * len(bits) * (1 if side is None else 0.5)),
        compiler_params=pltpu.CompilerParams(vmem_limit_bytes=8 << 20),
    )(*args)


def behind_kernel(bits, side, has_inv, has_acc, *refs):
    refs = list(refs)
    inv = refs.pop(0)[...] if has_inv else None
    img_ref = refs.pop(0)
    accs = [refs.pop(0) for _ in bits] if has_acc else [None] * len(bits)
    dh_ref, dl_ref = refs[:2]
    outs = refs[2:]
    vectors, _ = img_ref.shape
    half = vectors // 2
    real, imag = img_ref[:half], img_ref[half:]
    if has_inv:
        real, imag = exact(inv, real, NN), exact(inv, imag, NN)
    stacks = []
    for pair in ([real, imag], [imag, -real]):
        high, low = split(jnp.concatenate(pair, axis=0))
        stacks.append((high, jnp.concatenate([high, low], axis=0)))
    here = lax.axis_index("pix")
    rows = dh_ref.shape[1]
    span = pl.ds(side_start(side, rows), rows // 2)
    for b, acc, out in zip(bits, accs, outs):
        width = out.shape[1]
        col = pl.ds(pl.multiple_of((here ^ b) * width, width), width)
        wide = dot(stacks[0][1], dh_ref[0, span, col], NN) + dot(stacks[1][1], dh_ref[1, span, col], NN)
        low = dot(stacks[0][0], dl_ref[0, span, col], NN) + dot(stacks[1][0], dl_ref[1, span, col], NN)
        total = wide[:vectors] + wide[vectors:] + low
        out[...] = total if acc is None else total + acc[...]


def behind(images, bits, dh, dl, side, inv=None, accs=None):
    vectors = images.shape[0]
    width = dh.shape[2] // lax.axis_size("pix")
    args = ([] if inv is None else [inv]) + [images] + (list(accs) if accs else [])
    args += [in_vmem(dh), in_vmem(dl)]
    kernel = functools.partial(
        behind_kernel, tuple(bits), side, inv is not None, accs is not None
    )
    return pl.pallas_call(
        kernel,
        out_shape=[jax.ShapeDtypeStruct((vectors, width), F32) for _ in bits],
        in_specs=[VMEM] * len(args),
        out_specs=[VMEM] * len(bits),
        cost_estimate=cost(0.2 * len(bits)),
        compiler_params=pltpu.CompilerParams(vmem_limit_bytes=8 << 20),
    )(*args)


def cost(us):
    return pl.CostEstimate(flops=0, transcendentals=0, bytes_accessed=int(us * 3.5e6))


def start(phase_steps, idx, probes, frames, scale, cut):
    vectors, modes = probes.shape
    steps, rows, count = frames.shape
    planes = pltpu.VMEM((2, rows, count), BF16)
    hbm = pl.BlockSpec(memory_space=pltpu.HBM)
    return pl.pallas_call(
        functools.partial(start_kernel, scale, cut),
        out_shape=[
            planes,
            planes,
            jax.ShapeDtypeStruct((vectors, rows // 2 if cut else rows), F32),
            jax.ShapeDtypeStruct((8, HB), F32),
            jax.ShapeDtypeStruct((modes // count,), jnp.int32),
            jax.ShapeDtypeStruct((2 * vectors, count), BF16),
            jax.ShapeDtypeStruct((2 * vectors, count), BF16),
        ],
        in_specs=[hbm, hbm, hbm, hbm],
        out_specs=[VMEM, VMEM, VMEM, VMEM, SMEM, VMEM, VMEM],
        cost_estimate=cost(12),
        scratch_shapes=[
            pltpu.VMEM((steps, rows, count), F32),
            pltpu.VMEM((vectors, modes), F32),
            pltpu.VMEM((vectors, modes), F32),
            pltpu.VMEM((modes, HB), F32),
            pltpu.VMEM((count, HB), F32),
            pltpu.SMEM((modes,), jnp.int32),
            pltpu.SMEM((steps,), jnp.int32),
            pltpu.SemaphoreType.DMA((steps, rows // min(COPY, rows))),
            pltpu.SemaphoreType.DMA,
            pltpu.SemaphoreType.DMA((2,)),
        ],
        compiler_params=pltpu.CompilerParams(vmem_limit_bytes=44 << 20),
    )(*[pltpu.with_memory_space_constraint(x, pltpu.HBM) for x in (phase_steps, idx, probes, frames)])


def scatter_kernel(places, base_ref, idx_ref, *refs):
    s_ref, w_ref = refs[-1], refs[-2]
    pieces = [r for r in refs[:-2] if len(r.shape) == 2 and r.shape[1] == s_ref.shape[0]]
    count = s_ref.shape[0]
    for p, x_ref in enumerate(pieces):
        for i in range(count // HB):
            high, low = split(x_ref[:, i * HB : (i + 1) * HB])
            both = jnp.concatenate([high.astype(F32), low.astype(F32)], axis=0)
            s_ref[i * HB : (i + 1) * HB, :] = both.T
        base = base_ref[places[p]]

        def move(t, carry, base=base):
            at = pl.multiple_of(t * 32, 32)
            for q in range(32):
                w_ref[pl.ds(idx_ref[base + at + q], 1), :] = s_ref[pl.ds(at + q, 1), :]
            return carry

        lax.fori_loop(0, count // 32, move, 0)


def scatter_rows(places, bases, idx, pieces, table=None):
    count = pieces[0].shape[1]
    args = [bases, idx, *pieces] + ([] if table is None else [table])
    return pl.pallas_call(
        functools.partial(scatter_kernel, places),
        cost_estimate=cost(1.7 * len(pieces)),
        out_shape=jax.ShapeDtypeStruct((idx.shape[0], HB), F32),
        in_specs=[SMEM, SMEM] + [VMEM] * (len(args) - 2),
        out_specs=VMEM,
        scratch_shapes=[pltpu.VMEM((count, HB), F32)],
        input_output_aliases={} if table is None else {len(args) - 1: 0},
        compiler_params=pltpu.CompilerParams(vmem_limit_bytes=8 << 20),
    )(*args)


def end_kernel(inv_ref, w_ref, out_ref, y_ref, z_ref, o_ref, sems):
    vectors, modes = out_ref.shape
    half = vectors // 2
    outer = modes // HW
    signs = sign_table(HW).astype(BF16)
    zero = jnp.zeros((half, half), F32)
    wide = jnp.concatenate(
        [jnp.concatenate([inv_ref[...], zero], 1), jnp.concatenate([zero, inv_ref[...]], 1)], 0
    )
    high, low = split(wide)
    mix = jnp.concatenate(
        [jnp.concatenate([high, high], 1), jnp.concatenate([low, jnp.zeros_like(low)], 1)], 0
    )

    def first(i):
        at = pl.multiple_of(i * HW, HW)
        both = dot(mix, w_ref[pl.ds(at, HW), :].astype(BF16), NT)
        y_ref[:, pl.ds(at, HW)] = both[:vectors] + both[vectors:]

    block_loop(outer, 8, first)
    butterfly(y_ref, z_ref, outer, HW)
    per = modes // sems.shape[0]
    copies = [
        pltpu.make_async_copy(
            o_ref.at[:, pl.ds(c * per, per)], out_ref.at[:, pl.ds(c * per, per)], sems.at[c]
        )
        for c in range(sems.shape[0])
    ]
    for c, copy in enumerate(copies):
        for i in range(c * per, (c + 1) * per, HW):
            both = dot(jnp.concatenate(split(z_ref[:, i : i + HW]), axis=0), signs, NN)
            o_ref[:, i : i + HW] = both[:vectors] + both[vectors:]
        copy.start()
    for copy in copies:
        copy.wait()


def end_vectors(inv, table, vectors):
    return pl.pallas_call(
        end_kernel,
        cost_estimate=cost(6),
        out_shape=jax.ShapeDtypeStruct((vectors, table.shape[0]), F32),
        in_specs=[VMEM, VMEM],
        out_specs=pl.BlockSpec(memory_space=pltpu.HBM),
        scratch_shapes=[pltpu.VMEM((vectors, table.shape[0]), F32)] * 3
        + [pltpu.SemaphoreType.DMA((4,))],
        compiler_params=pltpu.CompilerParams(vmem_limit_bytes=14 << 20),
    )(inv, table)


def factor_kernel(g_ref, out_ref):
    n = out_ref.shape[0]
    eliminate(
        jnp.concatenate([g_ref[:, i * n : (i + 1) * n] for i in range(n // 8)], axis=0), out_ref
    )


def eliminate(square, out_ref):
    n = square.shape[0]
    row = lax.broadcasted_iota(jnp.int32, (n, n), 0)
    eye = (row == lax.broadcasted_iota(jnp.int32, (n, n), 1)).astype(F32)
    both = jnp.concatenate([square, eye], axis=1)
    below = lax.broadcasted_iota(jnp.int32, (n, 1), 0)
    for k in range(n - 1):
        scaled = both[k : k + 1] * (1.0 / both[k : k + 1, k : k + 1])
        both = both - jnp.where(below > k, both[:, k : k + 1], 0.0) * scaled
    pivots = jnp.sum(both[:, :n] * eye, axis=1, keepdims=True)
    out_ref[...] = both[:, n:] * (1.0 / jnp.sqrt(pivots))


def pack(gram_matrix):
    n = gram_matrix.shape[0]
    return jnp.concatenate([gram_matrix[i : i + 8] for i in range(0, n, 8)], axis=1)


def probe_factor_kernel(p_ref, out_ref):
    eliminate(gram(p_ref[...]), out_ref)


def probe_factor(probes):
    n = probes.shape[0] // 2
    return pl.pallas_call(
        probe_factor_kernel,
        out_shape=jax.ShapeDtypeStruct((n, n), F32),
        in_specs=[VMEM],
        out_specs=VMEM,
        cost_estimate=cost(4.5),
        compiler_params=pltpu.CompilerParams(vmem_limit_bytes=8 << 20),
    )(probes)


def inverse_factor(packed, n):
    return pl.pallas_call(
        factor_kernel,
        cost_estimate=cost(2.7),
        out_shape=jax.ShapeDtypeStruct((n, n), F32),
        in_specs=[VMEM],
        out_specs=VMEM,
        compiler_params=pltpu.CompilerParams(vmem_limit_bytes=2 << 20),
    )(packed)


def stack_forward(u):
    half = u.shape[0] // 2
    turned = jnp.concatenate([-u[half:], u[:half]], axis=0)
    uh, ul = split(u)
    th, tl = split(turned)
    return jnp.concatenate([uh, ul], axis=0), jnp.concatenate([th, tl], axis=0)


def apply_forward(both, turned, dh, dl, span):
    n = both.shape[0] // 2
    wide = dot(both, dh[0, span], NT) + dot(turned, dh[1, span], NT)
    low = dot(both[:n], dl[0, span], NT) + dot(turned[:n], dl[1, span], NT)
    return wide[:n] + wide[n:] + low


def gram(vectors):
    half = vectors.shape[0] // 2
    return exact(vectors[:half], vectors[:half], NT) + exact(vectors[half:], vectors[half:], NT)


def forward_kernel(u_ref, dh_ref, dl_ref, img_ref, gram_ref):
    gram_ref[...] = pack(gram(u_ref[...]))
    both, turned = stack_forward(u_ref[...])
    rows = dh_ref.shape[1]
    block = min(BLOCK, rows)
    width = img_ref.shape[-1]
    for i in range(rows // block):
        part = apply_forward(both, turned, dh_ref, dl_ref, slice(i * block, (i + 1) * block))
        if len(img_ref.shape) == 2:
            img_ref[:, i * block : (i + 1) * block] = part
        else:
            for j in range(block // width):
                img_ref[i * block // width + j] = part[:, j * width : (j + 1) * width]


def forward(u, dh, dl, places=None):
    rows = dh.shape[1]
    vectors = u.shape[0]
    shape = (vectors, rows) if places is None else (places, vectors, rows // places)
    return pl.pallas_call(
        forward_kernel,
        out_shape=[
            jax.ShapeDtypeStruct(shape, F32),
            jax.ShapeDtypeStruct((8, vectors // 2 * vectors // 16), F32),
        ],
        in_specs=[VMEM, VMEM, VMEM],
        out_specs=[VMEM, VMEM],
        cost_estimate=cost(2.7),
        compiler_params=pltpu.CompilerParams(vmem_limit_bytes=12 << 20),
    )(u, in_vmem(dh), in_vmem(dl))


def backward_kernel(*refs):
    inv_ref = refs[0] if len(refs) == 5 else None
    img_ref, dh_ref, dl_ref, ret_ref = refs[-4:]
    vectors, _ = img_ref.shape
    half = vectors // 2
    real, imag = img_ref[:half], img_ref[half:]
    if inv_ref is not None:
        real = exact(inv_ref[...], real, NN)
        imag = exact(inv_ref[...], imag, NN)
    stacks = []
    for pair in ([real, imag], [imag, -real]):
        high, low = split(jnp.concatenate(pair, axis=0))
        stacks.append((high, jnp.concatenate([high, low], axis=0)))
    cols = dh_ref.shape[2]
    block = min(BLOCK, cols)
    for i in range(cols // block):
        span = slice(i * block, (i + 1) * block)
        wide = dot(stacks[0][1], dh_ref[0, :, span], NN) + dot(stacks[1][1], dh_ref[1, :, span], NN)
        low = dot(stacks[0][0], dl_ref[0, :, span], NN) + dot(stacks[1][0], dl_ref[1, :, span], NN)
        ret_ref[:, span] = wide[:vectors] + wide[vectors:] + low


def backward(inv, images, dh, dl):
    args = ([] if inv is None else [inv]) + [images, in_vmem(dh), in_vmem(dl)]
    return pl.pallas_call(
        backward_kernel,
        cost_estimate=cost(1.6),
        out_shape=jax.ShapeDtypeStruct((images.shape[0], dh.shape[2]), F32),
        in_specs=[VMEM] * len(args),
        out_specs=VMEM,
        compiler_params=pltpu.CompilerParams(vmem_limit_bytes=12 << 20),
    )(*args)


def normalise(inv, vectors):
    half = inv.shape[0]
    return jnp.concatenate([exact(inv, vectors[:half], NN), exact(inv, vectors[half:], NN)], axis=0)


def flip(n, bit):
    return [(i, i ^ bit) for i in range(n)]


def pick(pieces, odds):
    for bit, odd in enumerate(odds):
        pieces = [jnp.where(odd, pieces[b ^ (1 << bit)], pieces[b]) for b in range(len(pieces))]
    return pieces


def scatter_sum(blocks, axis, step, odds):
    size = lax.axis_size(axis)
    mine = pick(blocks, odds)
    total = mine[0]
    for b in range(len(blocks) - 1, 0, -1):
        total = total + lax.ppermute(mine[b], axis, flip(size, b * step))
    return total


def gather_all(block, axis, step, odds):
    size = lax.axis_size(axis)
    far = [block]
    for b in range(1, 2 ** len(odds)):
        far.append(lax.ppermute(block, axis, flip(size, b * step)))
    return pick(far, odds)


def share_sum(block, axis, step, n):
    size = lax.axis_size(axis)
    total = block
    for b in range(n - 1, 0, -1):
        total = total + lax.ppermute(block, axis, flip(size, b * step))
    return total


def double_sum(block, axis):
    size = lax.axis_size(axis)
    bit = 1
    while bit < size:
        block = block + lax.ppermute(block, axis, flip(size, bit))
        bit *= 2
    return block


def sum_pix(x, odds):
    n = lax.axis_size("pix")
    if n != 4:
        return double_sum(x, "pix")
    rows = x.shape[0] // n
    odds = odds[4:6]
    blocks = [x[i * rows : (i + 1) * rows] for i in range(n)]
    mine = scatter_sum(blocks, "pix", 1, odds)
    return jnp.concatenate(gather_all(mine, "pix", 1, odds), axis=0)


def sum_mode(x, odds, extra=None):
    n = lax.axis_size("mode")
    rows, cols = x.shape
    if n != 8:
        small = None if extra is None else double_sum(extra, "mode")
        return double_sum(x, "mode"), small
    half = rows // 2
    odd = odds[0]
    mine = jnp.where(odd, x[half:], x[:half])
    other = jnp.where(odd, x[:half], x[half:])
    if extra is not None:
        width = extra.shape[1]
        row = jnp.pad(extra, ((0, 0), (0, cols - width)))
        mine = jnp.concatenate([mine, row], axis=0)
        other = jnp.concatenate([other, row], axis=0)
    chip = mine + lax.ppermute(other, "mode", flip(n, 1))
    chip = share_sum(chip, "mode", 2, 4)
    mine = chip[:half]
    other = lax.ppermute(mine, "mode", flip(n, 1))
    total = jnp.concatenate([jnp.where(odd, other, mine), jnp.where(odd, mine, other)], axis=0)
    return total, (None if extra is None else chip[half:, :width])


def scatter_mode(pieces, odds, extra):
    _, rows, width = pieces.shape
    n = lax.axis_size("mode")
    here = lax.axis_index("mode")
    if n != 8:
        total = double_sum(pieces, "mode")
        return lax.dynamic_index_in_dim(total, here, 0, False), double_sum(extra, "mode")
    odd = odds[0]
    mine = jnp.concatenate([jnp.where(odd, pieces[2 * i + 1], pieces[2 * i]) for i in range(4)])
    other = [jnp.where(odd, pieces[2 * i], pieces[2 * i + 1]) for i in range(4)]
    small = jnp.pad(extra, ((0, 0), (0, width - extra.shape[1])))
    got = lax.ppermute(jnp.concatenate(other + [small], axis=0), "mode", flip(n, 1))
    mine = mine + got[: 4 * rows]
    small = small + got[4 * rows :]
    blocks = [
        jnp.concatenate([mine[i * rows : (i + 1) * rows], small], axis=0) for i in range(4)
    ]
    total = scatter_sum(blocks, "mode", 2, odds[1:3])
    return total[:rows], total[rows:, : extra.shape[1]]


def gather_rows(block, bases, idx):
    n = lax.axis_size("mode")
    if n != 8:
        pieces = [block]
        bit = 1
        while bit < n:
            pieces = pieces + [lax.ppermute(p, "mode", flip(n, bit)) for p in pieces]
            bit *= 2
        return scatter_rows(range(n), bases, idx, pieces)
    got = {}
    for b in (6, 4, 2, 1):
        got[b] = lax.ppermute(block, "mode", flip(n, b))
    table = scatter_rows((0, 1), bases, idx, [block, got[1]])
    for b in (2, 4, 6):
        other = lax.ppermute(got[b], "mode", flip(n, 1))
        table = scatter_rows((b, b ^ 1), bases, idx, [got[b], other], table)
    return table


def sum_chips(other, own, packed=None):
    n = lax.axis_size("mode")
    rows = other.shape[0]
    if packed is not None:
        row = jnp.pad(packed, ((0, 0), (0, other.shape[1] - packed.shape[1])))
        other = jnp.concatenate([other, row], axis=0)
    got = lax.ppermute(other, "mode", flip(n, 1))
    own = own()
    if packed is not None:
        own = jnp.concatenate([own, row], axis=0)
    chip = share_sum(own + got, "mode", 2, 4)
    far = lax.ppermute(chip[:rows], "mode", flip(n, 1))
    return chip[:rows], far, (None if packed is None else chip[rows:, : packed.shape[1]])


def return_pieces(mine, far, dh, dl, inv=None):
    n = lax.axis_size("pix")
    near = behind(mine, range(n), dh, dl, "own", inv)
    third, second = behind(far, (3, 2), dh, dl, "other", inv, (near[3], near[2]))
    first, total = behind(far, (1, 0), dh, dl, "other", inv, (near[1], near[0]))
    for b, piece in ((3, third), (2, second), (1, first)):
        total = total + lax.ppermute(piece, "pix", flip(n, b))
    out = [total]
    for b in (1, 2, 3):
        out.append(lax.ppermute(total, "pix", flip(n, b)))
    return out


def measure(frames, phase_steps, pattern_rows, probes):
    columns = frames.shape[2]
    rows = frames.shape[1]
    groups = lax.axis_size("mode")
    places = lax.axis_size("pix")
    pixels = rows * places
    modes_total = columns * groups
    k = probes.shape[1]
    vectors = 2 * k
    probes = probes.reshape(vectors, modes_total)
    scale = 1.0 / math.sqrt(modes_total)
    cut = groups == 8 and places == 4
    dh, dl, images, masks, bases, both, turned = start(
        phase_steps, pattern_rows, probes, frames, scale, cut
    )
    odds = [masks[b : b + 1, :1] != 0 for b in range(8)]
    inv = probe_factor(probes)
    if cut:
        mine, far, _ = sum_chips(images, lambda: own_half(both, turned, dh, dl))
        pieces = return_pieces(mine, far, dh, dl, inv)
        inv = None
        for iteration in range(1, ITERS + 1):
            early = ahead(pieces[:2], (0, 1), dh, dl, inv=inv)
            if iteration == ITERS:
                break
            other, packed = ahead(pieces[2:], (2, 3), dh, dl, "other", inv, early)

            def own(pieces=pieces, inv=inv, early=early):
                return ahead(pieces[2:], (2, 3), dh, dl, "own", inv, early, None, False)[0]

            mine, far, packed = sum_chips(other, own, packed)
            last_inv = inverse_factor(packed, k)
            pieces = return_pieces(mine, far, dh, dl, inv)
            inv = last_inv
        by_place = jnp.concatenate(pick(pieces, odds[4:6]), axis=1)
        returned = by_place if inv is None else normalise(inv, by_place)
        table = gather_rows(returned, bases, pattern_rows)
        images, packed = ahead(pieces[2:], (2, 3), dh, dl, None, inv, early, groups)
    else:
        images, _ = sum_mode(images, odds)
        returned = sum_pix(backward(inv, images, dh, dl), odds)
        for _ in range(1, ITERS):
            images, packed = forward(returned, dh, dl)
            images, packed = sum_mode(images, odds, packed)
            inv = inverse_factor(packed, k)
            partial = backward(None, images, dh, dl)
            returned = normalise(inv, sum_pix(partial, odds))
        table = gather_rows(returned, bases, pattern_rows)
        images, packed = forward(returned, dh, dl, groups)
    fields, packed = scatter_mode(images, odds, packed)
    inv = inverse_factor(packed, k)
    fields = normalise(inv, fields)
    power = jnp.sum(fields * fields, axis=1)
    power = jnp.broadcast_to((power[:k] + power[k:])[None, :], (8, k))
    power = double_sum(double_sum(power, "mode"), "pix")
    strengths = power[0] / pixels
    channels = end_vectors(inv, table, vectors)
    return (channels.reshape(2, k, modes_total), fields.reshape(2, k, -1), strengths)


def solution(mesh):
    in_specs = (P(None, "pix", "mode"), P(), P(), P())
    out_specs = (P(), P(None, None, ("pix", "mode")), P())
    return jax.shard_map(
        measure, mesh=mesh, in_specs=in_specs, out_specs=out_specs, check_vma=False
    )
```

```python
import functools
import math

import jax
import jax.numpy as jnp
from jax import lax
from jax.experimental import pallas as pl
from jax.experimental.pallas import tpu as pltpu
from jax.sharding import PartitionSpec as P

HB = 128
ITERS = 2
BLOCK = 256
HW = 256
COPY = 512
F32 = jnp.float32
BF16 = jnp.bfloat16

precise = lax.Precision.HIGHEST
NT = (((1,), (1,)), ((), ()))
NN = (((1,), (0,)), ((), ()))
VMEM = pl.BlockSpec(memory_space=pltpu.VMEM)
SMEM = pl.BlockSpec(memory_space=pltpu.SMEM)


def dot(a, b, dims):
    return lax.dot_general(a, b, dims, preferred_element_type=F32)


def exact(a, b, dims):
    return lax.dot_general(a, b, dims, precision=precise, preferred_element_type=F32)


def in_vmem(x):
    return pltpu.with_memory_space_constraint(x, pltpu.VMEM)


def split(values):
    high = values.astype(BF16)
    return high, (values - high.astype(F32)).astype(BF16)


def sign_table(order):
    row = lax.broadcasted_iota(jnp.int32, (order, order), 0)
    common = row & lax.broadcasted_iota(jnp.int32, (order, order), 1)
    parity = common
    shift = 16
    while shift:
        parity = parity ^ (parity >> shift)
        shift //= 2
    return (1 - 2 * (parity & 1)).astype(F32)


def butterfly(src, dst, count, width):
    rows = src.shape[0]
    step = 1
    while step < count:
        radix = min(32, count // step)
        for g in range(count // radix):
            base = (g // step) * (step * radix) + g % step
            for s in range(0, rows, 8):
                for lane in range(0, width, HB):
                    at = [(base + r * step) * width + lane for r in range(radix)]
                    v = [src[s : s + 8, a : a + HB] for a in at]
                    half = 1
                    while half < radix:
                        v = [
                            v[r] + v[r + half] if not r & half else v[r - half] - v[r]
                            for r in range(radix)
                        ]
                        half *= 2
                    for a, x in zip(at, v):
                        dst[s : s + 8, a : a + HB] = x
        step *= radix
        src = dst


def block_loop(count, unroll, body):
    unroll = math.gcd(count, unroll)

    def many(i, carry):
        for q in range(unroll):
            body(i * unroll + q)
        return carry

    lax.fori_loop(0, count // unroll, many, 0)


def start_kernel(
    scale, cut, phase_ref, rows_ref, probes_ref, frames_ref,
    dh_ref, dl_ref, img_ref, mask_ref, base_ref, b_ref, t_ref, f_ref, p_ref, w_ref, n_ref, g_ref,
    idx_ref, steps_ref,
    sems, sem, tiny,
):
    vectors, modes = probes_ref.shape
    steps, rows, count = frames_ref.shape
    outer = modes // HW
    block = min(COPY, rows)
    small = [
        pltpu.make_async_copy(rows_ref, idx_ref, tiny.at[0]),
        pltpu.make_async_copy(phase_ref, steps_ref, tiny.at[1]),
    ]
    for c in small:
        c.start()
    first = pltpu.make_async_copy(probes_ref, p_ref, sem)
    first.start()
    copies = [
        [
            pltpu.make_async_copy(
                frames_ref.at[s, pl.ds(i * block, block)],
                f_ref.at[s, pl.ds(i * block, block)],
                sems.at[s, i],
            )
            for s in range(steps)
        ]
        for i in range(rows // block)
    ]
    here = (lax.axis_index("mode"), lax.axis_index("pix"))
    for b in range(4):
        for place, axis_row in ((here[0], 0), (here[1], 4)):
            bit = ((place >> b) & 1).astype(F32)
            mask_ref[axis_row + b : axis_row + b + 1, :] = jnp.full((1, HB), bit, F32)
    for b in range(base_ref.shape[0]):
        base_ref[b] = (here[0] ^ b) * count
    signs = sign_table(HW).astype(BF16)
    first.wait()
    half = (len(copies) + 1) // 2
    for row in copies[:half]:
        for c in row:
            c.start()
    butterfly(p_ref, w_ref, outer, HW)

    def inner(i):
        at = pl.multiple_of(i * HW, HW)
        both = jnp.concatenate(split(w_ref[:, pl.ds(at, HW)]), axis=0)
        n_ref[pl.ds(at, HW), :] = dot(signs, both, NT)

    block_loop(outer, 8, inner)
    for row in copies[half:]:
        for c in row:
            c.start()
    start_at = here[0] * count
    small[0].wait()

    def gather(t, carry):
        at = pl.multiple_of(t * 32, 32)
        for q in range(32):
            g_ref[pl.ds(at + q, 1), :] = n_ref[pl.ds(idx_ref[start_at + at + q], 1), :]
        return carry

    lax.fori_loop(0, count // 32, gather, 0)
    parts = [g_ref[b * HB : (b + 1) * HB, :].T for b in range(count // HB)]
    parts = [p[:vectors] + p[vectors:] for p in parts]
    b_ref[...], t_ref[...] = stack_forward(jnp.concatenate(parts, axis=1) * scale)
    small[1].wait()
    frame = [
        sum(jnp.where(steps_ref[f] == s, f, 0) for f in range(1, steps)) for s in range(steps)
    ]
    for i, row in enumerate(copies):
        for c in row:
            c.wait()
        span = slice(i * block, (i + 1) * block)
        for part in (0, 1):
            high, low = split(0.25 * (f_ref[frame[part], span] - f_ref[frame[part + 2], span]))
            dh_ref[part, span] = high
            dl_ref[part, span] = low
        if not cut:
            img_ref[:, span] = apply_forward(b_ref[...], t_ref[...], dh_ref, dl_ref, span)
    if cut:
        from_rows(img_ref, "other", b_ref[...], t_ref[...], dh_ref, dl_ref)


def side_start(side, rows):
    core = lax.axis_index("mode") & 1
    return pl.multiple_of((core if side == "own" else 1 - core) * (rows // 2), rows // 2)


def from_rows(img_ref, side, both, turned, dh_ref, dl_ref):
    rows = dh_ref.shape[1]
    base = side_start(side, rows)
    for i in range(0, rows // 2, BLOCK):
        span = pl.ds(base + i, BLOCK)
        img_ref[:, i : i + BLOCK] = apply_forward(both, turned, dh_ref, dl_ref, span)


def own_kernel(b_ref, t_ref, dh_ref, dl_ref, img_ref):
    from_rows(img_ref, "own", b_ref[...], t_ref[...], dh_ref, dl_ref)


def own_half(both, turned, dh, dl):
    return pl.pallas_call(
        own_kernel,
        out_shape=jax.ShapeDtypeStruct((both.shape[0] // 2, dh.shape[1] // 2), F32),
        in_specs=[VMEM] * 4,
        out_specs=VMEM,
        cost_estimate=cost(1.3),
        compiler_params=pltpu.CompilerParams(vmem_limit_bytes=8 << 20),
    )(both, turned, in_vmem(dh), in_vmem(dl))


def ahead_kernel(bits, side, has_inv, has_acc, places, *refs):
    refs = list(refs)
    inv = refs.pop(0)[...] if has_inv else None
    acc_ref, acc_gram = (refs.pop(0), refs.pop(0)) if has_acc else (None, None)
    pieces = [refs.pop(0)[...] for _ in bits]
    dh_ref, dl_ref, img_ref = refs[:3]
    here = lax.axis_index("pix")
    width = pieces[0].shape[1]
    half = pieces[0].shape[0] // 2
    if has_inv:
        pieces = [
            jnp.concatenate([exact(inv, p[:half], NN), exact(inv, p[half:], NN)], axis=0)
            for p in pieces
        ]
    if len(refs) > 3:
        total = pack(sum(gram(p) for p in pieces))
        refs[3][...] = total if acc_gram is None else total + acc_gram[...]
    stacks = [stack_forward(p) for p in pieces]
    cols = [pl.ds(pl.multiple_of((here ^ b) * width, width), width) for b in bits]
    rows = dh_ref.shape[1]
    base = 0 if side is None else side_start(side, rows)
    for i in range(0, rows if side is None else rows // 2, BLOCK):
        span = pl.ds(base + i, BLOCK)
        part = sum(apply_ahead(*st, dh_ref, dl_ref, span, col) for st, col in zip(stacks, cols))
        if acc_ref is not None:
            part = part + acc_ref[:, span]
        if places is None:
            img_ref[:, i : i + BLOCK] = part
        else:
            w = rows // places
            chip = lax.axis_index("mode") >> 1
            core = lax.axis_index("mode") & 1
            for j in range(BLOCK // w):
                p = i // w + j
                slot = ((p & 1) ^ core) * (places // 2) + ((p >> 1) ^ chip)
                img_ref[slot] = part[:, j * w : (j + 1) * w]


def apply_ahead(both, turned, dh, dl, span, col):
    n = both.shape[0] // 2
    wide = dot(both, dh[0, span, col], NT) + dot(turned, dh[1, span, col], NT)
    low = dot(both[:n], dl[0, span, col], NT) + dot(turned[:n], dl[1, span, col], NT)
    return wide[:n] + wide[n:] + low


def ahead(pieces, bits, dh, dl, side=None, inv=None, acc=None, places=None, with_gram=True):
    rows = dh.shape[1]
    vectors = pieces[0].shape[0]
    shape = (vectors, rows if side is None else rows // 2)
    if places is not None:
        shape = (places, vectors, rows // places)
    out = [jax.ShapeDtypeStruct(shape, F32)]
    if with_gram:
        out.append(jax.ShapeDtypeStruct((8, vectors // 2 * vectors // 16), F32))
    args = ([] if inv is None else [inv]) + (list(acc) if acc else []) + list(pieces)
    args += [in_vmem(dh), in_vmem(dl)]
    kernel = functools.partial(
        ahead_kernel, tuple(bits), side, inv is not None, acc is not None, places
    )
    return pl.pallas_call(
        kernel,
        out_shape=out,
        in_specs=[VMEM] * len(args),
        out_specs=[VMEM] * len(out),
        cost_estimate=cost(0.7 * len(bits) * (1 if side is None else 0.5)),
        compiler_params=pltpu.CompilerParams(vmem_limit_bytes=8 << 20),
    )(*args)


def join_kernel(inv_ref, *refs):
    out_ref = refs[-1]
    here = lax.axis_index("pix")
    half = out_ref.shape[0] // 2
    for b, ref in enumerate(refs[:-1]):
        width = ref.shape[1]
        col = pl.ds(pl.multiple_of((here ^ b) * width, width), width)
        out_ref[:half, col] = exact(inv_ref[...], ref[:half], NN)
        out_ref[half:, col] = exact(inv_ref[...], ref[half:], NN)


def join(inv, pieces):
    vectors, width = pieces[0].shape
    return pl.pallas_call(
        join_kernel,
        out_shape=jax.ShapeDtypeStruct((vectors, width * len(pieces)), F32),
        in_specs=[VMEM] * (1 + len(pieces)),
        out_specs=VMEM,
        cost_estimate=cost(0.5),
        compiler_params=pltpu.CompilerParams(vmem_limit_bytes=4 << 20),
    )(inv, *pieces)


def behind_kernel(bits, side, has_inv, has_acc, *refs):
    refs = list(refs)
    inv = refs.pop(0)[...] if has_inv else None
    img_ref = refs.pop(0)
    accs = [refs.pop(0) for _ in bits] if has_acc else [None] * len(bits)
    dh_ref, dl_ref = refs[:2]
    outs = refs[2:]
    vectors, _ = img_ref.shape
    half = vectors // 2
    real, imag = img_ref[:half], img_ref[half:]
    if has_inv:
        real, imag = exact(inv, real, NN), exact(inv, imag, NN)
    stacks = []
    for pair in ([real, imag], [imag, -real]):
        high, low = split(jnp.concatenate(pair, axis=0))
        stacks.append((high, jnp.concatenate([high, low], axis=0)))
    here = lax.axis_index("pix")
    rows = dh_ref.shape[1]
    span = pl.ds(side_start(side, rows), rows // 2)
    for b, acc, out in zip(bits, accs, outs):
        width = out.shape[1]
        col = pl.ds(pl.multiple_of((here ^ b) * width, width), width)
        wide = dot(stacks[0][1], dh_ref[0, span, col], NN) + dot(stacks[1][1], dh_ref[1, span, col], NN)
        low = dot(stacks[0][0], dl_ref[0, span, col], NN) + dot(stacks[1][0], dl_ref[1, span, col], NN)
        total = wide[:vectors] + wide[vectors:] + low
        out[...] = total if acc is None else total + acc[...]


def behind(images, bits, dh, dl, side, inv=None, accs=None):
    vectors = images.shape[0]
    width = dh.shape[2] // lax.axis_size("pix")
    args = ([] if inv is None else [inv]) + [images] + (list(accs) if accs else [])
    args += [in_vmem(dh), in_vmem(dl)]
    kernel = functools.partial(
        behind_kernel, tuple(bits), side, inv is not None, accs is not None
    )
    return pl.pallas_call(
        kernel,
        out_shape=[jax.ShapeDtypeStruct((vectors, width), F32) for _ in bits],
        in_specs=[VMEM] * len(args),
        out_specs=[VMEM] * len(bits),
        cost_estimate=cost(0.2 * len(bits)),
        compiler_params=pltpu.CompilerParams(vmem_limit_bytes=8 << 20),
    )(*args)


def cost(us):
    return pl.CostEstimate(flops=0, transcendentals=0, bytes_accessed=int(us * 3.5e6))


def start(phase_steps, idx, probes, frames, scale, cut):
    vectors, modes = probes.shape
    steps, rows, count = frames.shape
    planes = pltpu.VMEM((2, rows, count), BF16)
    hbm = pl.BlockSpec(memory_space=pltpu.HBM)
    return pl.pallas_call(
        functools.partial(start_kernel, scale, cut),
        out_shape=[
            planes,
            planes,
            jax.ShapeDtypeStruct((vectors, rows // 2 if cut else rows), F32),
            jax.ShapeDtypeStruct((8, HB), F32),
            jax.ShapeDtypeStruct((modes // count,), jnp.int32),
            jax.ShapeDtypeStruct((2 * vectors, count), BF16),
            jax.ShapeDtypeStruct((2 * vectors, count), BF16),
        ],
        in_specs=[hbm, hbm, hbm, hbm],
        out_specs=[VMEM, VMEM, VMEM, VMEM, SMEM, VMEM, VMEM],
        cost_estimate=cost(12),
        scratch_shapes=[
            pltpu.VMEM((steps, rows, count), F32),
            pltpu.VMEM((vectors, modes), F32),
            pltpu.VMEM((vectors, modes), F32),
            pltpu.VMEM((modes, HB), F32),
            pltpu.VMEM((count, HB), F32),
            pltpu.SMEM((modes,), jnp.int32),
            pltpu.SMEM((steps,), jnp.int32),
            pltpu.SemaphoreType.DMA((steps, rows // min(COPY, rows))),
            pltpu.SemaphoreType.DMA,
            pltpu.SemaphoreType.DMA((2,)),
        ],
        compiler_params=pltpu.CompilerParams(vmem_limit_bytes=44 << 20),
    )(*[pltpu.with_memory_space_constraint(x, pltpu.HBM) for x in (phase_steps, idx, probes, frames)])


def scatter_kernel(places, base_ref, idx_ref, *refs):
    s_ref, w_ref = refs[-1], refs[-2]
    pieces = [r for r in refs[:-2] if len(r.shape) == 2 and r.shape[1] == s_ref.shape[0]]
    count = s_ref.shape[0]
    for p, x_ref in enumerate(pieces):
        for i in range(count // HB):
            high, low = split(x_ref[:, i * HB : (i + 1) * HB])
            both = jnp.concatenate([high.astype(F32), low.astype(F32)], axis=0)
            s_ref[i * HB : (i + 1) * HB, :] = both.T
        base = base_ref[places[p]]

        def move(t, carry, base=base):
            at = pl.multiple_of(t * 32, 32)
            for q in range(32):
                w_ref[pl.ds(idx_ref[base + at + q], 1), :] = s_ref[pl.ds(at + q, 1), :]
            return carry

        lax.fori_loop(0, count // 32, move, 0)


def scatter_rows(places, bases, idx, pieces, table=None):
    count = pieces[0].shape[1]
    args = [bases, idx, *pieces] + ([] if table is None else [table])
    return pl.pallas_call(
        functools.partial(scatter_kernel, places),
        cost_estimate=cost(1.7 * len(pieces)),
        out_shape=jax.ShapeDtypeStruct((idx.shape[0], HB), F32),
        in_specs=[SMEM, SMEM] + [VMEM] * (len(args) - 2),
        out_specs=VMEM,
        scratch_shapes=[pltpu.VMEM((count, HB), F32)],
        input_output_aliases={} if table is None else {len(args) - 1: 0},
        compiler_params=pltpu.CompilerParams(vmem_limit_bytes=8 << 20),
    )(*args)


def end_kernel(inv_ref, w_ref, out_ref, y_ref, z_ref, o_ref, sems):
    vectors, modes = out_ref.shape
    half = vectors // 2
    outer = modes // HW
    signs = sign_table(HW).astype(BF16)
    zero = jnp.zeros((half, half), F32)
    wide = jnp.concatenate(
        [jnp.concatenate([inv_ref[...], zero], 1), jnp.concatenate([zero, inv_ref[...]], 1)], 0
    )
    high, low = split(wide)
    mix = jnp.concatenate(
        [jnp.concatenate([high, high], 1), jnp.concatenate([low, jnp.zeros_like(low)], 1)], 0
    )

    def first(i):
        at = pl.multiple_of(i * HW, HW)
        both = dot(mix, w_ref[pl.ds(at, HW), :].astype(BF16), NT)
        y_ref[:, pl.ds(at, HW)] = both[:vectors] + both[vectors:]

    block_loop(outer, 8, first)
    butterfly(y_ref, z_ref, outer, HW)
    per = modes // sems.shape[0]
    copies = [
        pltpu.make_async_copy(
            o_ref.at[:, pl.ds(c * per, per)], out_ref.at[:, pl.ds(c * per, per)], sems.at[c]
        )
        for c in range(sems.shape[0])
    ]
    for c, copy in enumerate(copies):
        for i in range(c * per, (c + 1) * per, HW):
            both = dot(jnp.concatenate(split(z_ref[:, i : i + HW]), axis=0), signs, NN)
            o_ref[:, i : i + HW] = both[:vectors] + both[vectors:]
        copy.start()
    for copy in copies:
        copy.wait()


def end_vectors(inv, table, vectors):
    return pl.pallas_call(
        end_kernel,
        cost_estimate=cost(6),
        out_shape=jax.ShapeDtypeStruct((vectors, table.shape[0]), F32),
        in_specs=[VMEM, VMEM],
        out_specs=pl.BlockSpec(memory_space=pltpu.HBM),
        scratch_shapes=[pltpu.VMEM((vectors, table.shape[0]), F32)] * 3
        + [pltpu.SemaphoreType.DMA((4,))],
        compiler_params=pltpu.CompilerParams(vmem_limit_bytes=14 << 20),
    )(inv, table)


def factor_kernel(g_ref, out_ref):
    n = out_ref.shape[0]
    eliminate(
        jnp.concatenate([g_ref[:, i * n : (i + 1) * n] for i in range(n // 8)], axis=0), out_ref
    )


def eliminate(square, out_ref):
    n = square.shape[0]
    row = lax.broadcasted_iota(jnp.int32, (n, n), 0)
    eye = (row == lax.broadcasted_iota(jnp.int32, (n, n), 1)).astype(F32)
    both = jnp.concatenate([square, eye], axis=1)
    below = lax.broadcasted_iota(jnp.int32, (n, 1), 0)
    for k in range(n - 1):
        scaled = both[k : k + 1] * (1.0 / both[k : k + 1, k : k + 1])
        both = both - jnp.where(below > k, both[:, k : k + 1], 0.0) * scaled
    pivots = jnp.sum(both[:, :n] * eye, axis=1, keepdims=True)
    out_ref[...] = both[:, n:] * (1.0 / jnp.sqrt(pivots))


def pack(gram_matrix):
    n = gram_matrix.shape[0]
    return jnp.concatenate([gram_matrix[i : i + 8] for i in range(0, n, 8)], axis=1)


def probe_factor_kernel(p_ref, out_ref):
    eliminate(gram(p_ref[...]), out_ref)


def probe_factor(probes):
    n = probes.shape[0] // 2
    return pl.pallas_call(
        probe_factor_kernel,
        out_shape=jax.ShapeDtypeStruct((n, n), F32),
        in_specs=[VMEM],
        out_specs=VMEM,
        cost_estimate=cost(4.5),
        compiler_params=pltpu.CompilerParams(vmem_limit_bytes=8 << 20),
    )(probes)


def inverse_factor(packed, n):
    return pl.pallas_call(
        factor_kernel,
        cost_estimate=cost(2.7),
        out_shape=jax.ShapeDtypeStruct((n, n), F32),
        in_specs=[VMEM],
        out_specs=VMEM,
        compiler_params=pltpu.CompilerParams(vmem_limit_bytes=2 << 20),
    )(packed)


def stack_forward(u):
    half = u.shape[0] // 2
    turned = jnp.concatenate([-u[half:], u[:half]], axis=0)
    uh, ul = split(u)
    th, tl = split(turned)
    return jnp.concatenate([uh, ul], axis=0), jnp.concatenate([th, tl], axis=0)


def apply_forward(both, turned, dh, dl, span):
    n = both.shape[0] // 2
    wide = dot(both, dh[0, span], NT) + dot(turned, dh[1, span], NT)
    low = dot(both[:n], dl[0, span], NT) + dot(turned[:n], dl[1, span], NT)
    return wide[:n] + wide[n:] + low


def gram(vectors):
    half = vectors.shape[0] // 2
    return exact(vectors[:half], vectors[:half], NT) + exact(vectors[half:], vectors[half:], NT)


def forward_kernel(u_ref, dh_ref, dl_ref, img_ref, gram_ref):
    gram_ref[...] = pack(gram(u_ref[...]))
    both, turned = stack_forward(u_ref[...])
    rows = dh_ref.shape[1]
    block = min(BLOCK, rows)
    width = img_ref.shape[-1]
    for i in range(rows // block):
        part = apply_forward(both, turned, dh_ref, dl_ref, slice(i * block, (i + 1) * block))
        if len(img_ref.shape) == 2:
            img_ref[:, i * block : (i + 1) * block] = part
        else:
            for j in range(block // width):
                img_ref[i * block // width + j] = part[:, j * width : (j + 1) * width]


def forward(u, dh, dl, places=None):
    rows = dh.shape[1]
    vectors = u.shape[0]
    shape = (vectors, rows) if places is None else (places, vectors, rows // places)
    return pl.pallas_call(
        forward_kernel,
        out_shape=[
            jax.ShapeDtypeStruct(shape, F32),
            jax.ShapeDtypeStruct((8, vectors // 2 * vectors // 16), F32),
        ],
        in_specs=[VMEM, VMEM, VMEM],
        out_specs=[VMEM, VMEM],
        cost_estimate=cost(2.7),
        compiler_params=pltpu.CompilerParams(vmem_limit_bytes=12 << 20),
    )(u, in_vmem(dh), in_vmem(dl))


def backward_kernel(*refs):
    inv_ref = refs[0] if len(refs) == 5 else None
    img_ref, dh_ref, dl_ref, ret_ref = refs[-4:]
    vectors, _ = img_ref.shape
    half = vectors // 2
    real, imag = img_ref[:half], img_ref[half:]
    if inv_ref is not None:
        real = exact(inv_ref[...], real, NN)
        imag = exact(inv_ref[...], imag, NN)
    stacks = []
    for pair in ([real, imag], [imag, -real]):
        high, low = split(jnp.concatenate(pair, axis=0))
        stacks.append((high, jnp.concatenate([high, low], axis=0)))
    cols = dh_ref.shape[2]
    block = min(BLOCK, cols)
    for i in range(cols // block):
        span = slice(i * block, (i + 1) * block)
        wide = dot(stacks[0][1], dh_ref[0, :, span], NN) + dot(stacks[1][1], dh_ref[1, :, span], NN)
        low = dot(stacks[0][0], dl_ref[0, :, span], NN) + dot(stacks[1][0], dl_ref[1, :, span], NN)
        ret_ref[:, span] = wide[:vectors] + wide[vectors:] + low


def backward(inv, images, dh, dl):
    args = ([] if inv is None else [inv]) + [images, in_vmem(dh), in_vmem(dl)]
    return pl.pallas_call(
        backward_kernel,
        cost_estimate=cost(1.6),
        out_shape=jax.ShapeDtypeStruct((images.shape[0], dh.shape[2]), F32),
        in_specs=[VMEM] * len(args),
        out_specs=VMEM,
        compiler_params=pltpu.CompilerParams(vmem_limit_bytes=12 << 20),
    )(*args)


def normalise(inv, vectors):
    half = inv.shape[0]
    return jnp.concatenate([exact(inv, vectors[:half], NN), exact(inv, vectors[half:], NN)], axis=0)


def flip(n, bit):
    return [(i, i ^ bit) for i in range(n)]


def pick(pieces, odds):
    for bit, odd in enumerate(odds):
        pieces = [jnp.where(odd, pieces[b ^ (1 << bit)], pieces[b]) for b in range(len(pieces))]
    return pieces


def scatter_sum(blocks, axis, step, odds):
    size = lax.axis_size(axis)
    mine = pick(blocks, odds)
    total = mine[0]
    for b in range(len(blocks) - 1, 0, -1):
        total = total + lax.ppermute(mine[b], axis, flip(size, b * step))
    return total


def gather_all(block, axis, step, odds):
    size = lax.axis_size(axis)
    far = [block]
    for b in range(1, 2 ** len(odds)):
        far.append(lax.ppermute(block, axis, flip(size, b * step)))
    return pick(far, odds)


def share_sum(block, axis, step, n):
    size = lax.axis_size(axis)
    total = block
    for b in range(n - 1, 0, -1):
        total = total + lax.ppermute(block, axis, flip(size, b * step))
    return total


def double_sum(block, axis):
    size = lax.axis_size(axis)
    bit = 1
    while bit < size:
        block = block + lax.ppermute(block, axis, flip(size, bit))
        bit *= 2
    return block


def sum_pix(x, odds):
    n = lax.axis_size("pix")
    if n != 4:
        return double_sum(x, "pix")
    rows = x.shape[0] // n
    odds = odds[4:6]
    blocks = [x[i * rows : (i + 1) * rows] for i in range(n)]
    mine = scatter_sum(blocks, "pix", 1, odds)
    return jnp.concatenate(gather_all(mine, "pix", 1, odds), axis=0)


def sum_mode(x, odds, extra=None):
    n = lax.axis_size("mode")
    rows, cols = x.shape
    if n != 8:
        small = None if extra is None else double_sum(extra, "mode")
        return double_sum(x, "mode"), small
    half = rows // 2
    odd = odds[0]
    mine = jnp.where(odd, x[half:], x[:half])
    other = jnp.where(odd, x[:half], x[half:])
    if extra is not None:
        width = extra.shape[1]
        row = jnp.pad(extra, ((0, 0), (0, cols - width)))
        mine = jnp.concatenate([mine, row], axis=0)
        other = jnp.concatenate([other, row], axis=0)
    chip = mine + lax.ppermute(other, "mode", flip(n, 1))
    chip = share_sum(chip, "mode", 2, 4)
    mine = chip[:half]
    other = lax.ppermute(mine, "mode", flip(n, 1))
    total = jnp.concatenate([jnp.where(odd, other, mine), jnp.where(odd, mine, other)], axis=0)
    return total, (None if extra is None else chip[half:, :width])


def scatter_mode(pieces, extra):
    places, rows, width = pieces.shape
    n = lax.axis_size("mode")
    here = lax.axis_index("mode")
    if n != 8:
        total = double_sum(pieces, "mode")
        return lax.dynamic_index_in_dim(total, here, 0, False), double_sum(extra, "mode")
    small = jnp.pad(extra, ((0, 0), (0, width - extra.shape[1])))
    flat = pieces.reshape(places * rows, width)
    cut = 4 * rows
    got = lax.ppermute(
        jnp.concatenate([flat[cut:], small], axis=0), "mode", flip(n, 1)
    )
    mine = flat[:cut] + got[:cut]
    small = small + got[cut:]
    total = jnp.concatenate([mine[:rows], small], axis=0)
    for b in (3, 2, 1):
        block = jnp.concatenate([mine[b * rows : (b + 1) * rows], small], axis=0)
        total = total + lax.ppermute(block, "mode", flip(n, 2 * b))
    return total[:rows], total[rows:, : extra.shape[1]]


def gather_rows(block, bases, idx):
    n = lax.axis_size("mode")
    if n != 8:
        pieces = [block]
        bit = 1
        while bit < n:
            pieces = pieces + [lax.ppermute(p, "mode", flip(n, bit)) for p in pieces]
            bit *= 2
        return scatter_rows(range(n), bases, idx, pieces)
    got = {}
    for b in (6, 4, 2, 1):
        got[b] = lax.ppermute(block, "mode", flip(n, b))
    table = scatter_rows((0, 1), bases, idx, [block, got[1]])
    for b in (2, 4, 6):
        other = lax.ppermute(got[b], "mode", flip(n, 1))
        table = scatter_rows((b, b ^ 1), bases, idx, [got[b], other], table)
    return table


def sum_chips(other, own, packed=None):
    n = lax.axis_size("mode")
    rows = other.shape[0]
    if packed is not None:
        row = jnp.pad(packed, ((0, 0), (0, other.shape[1] - packed.shape[1])))
        other = jnp.concatenate([other, row], axis=0)
    got = lax.ppermute(other, "mode", flip(n, 1))
    own = own()
    if packed is not None:
        own = jnp.concatenate([own, row], axis=0)
    chip = share_sum(own + got, "mode", 2, 4)
    far = lax.ppermute(chip[:rows], "mode", flip(n, 1))
    return chip[:rows], far, (None if packed is None else chip[rows:, : packed.shape[1]])


def return_pieces(mine, far, dh, dl, inv=None):
    n = lax.axis_size("pix")
    near = behind(mine, range(n), dh, dl, "own", inv)
    third, second = behind(far, (3, 2), dh, dl, "other", inv, (near[3], near[2]))
    first, total = behind(far, (1, 0), dh, dl, "other", inv, (near[1], near[0]))
    for b, piece in ((3, third), (2, second), (1, first)):
        total = total + lax.ppermute(piece, "pix", flip(n, b))
    out = [total]
    for b in (1, 2, 3):
        out.append(lax.ppermute(total, "pix", flip(n, b)))
    return out


def measure(frames, phase_steps, pattern_rows, probes):
    columns = frames.shape[2]
    rows = frames.shape[1]
    groups = lax.axis_size("mode")
    places = lax.axis_size("pix")
    pixels = rows * places
    modes_total = columns * groups
    k = probes.shape[1]
    vectors = 2 * k
    probes = probes.reshape(vectors, modes_total)
    scale = 1.0 / math.sqrt(modes_total)
    cut = groups == 8 and places == 4
    dh, dl, images, masks, bases, both, turned = start(
        phase_steps, pattern_rows, probes, frames, scale, cut
    )
    inv = probe_factor(probes)
    if cut:
        mine, far, _ = sum_chips(images, lambda: own_half(both, turned, dh, dl))
        pieces = return_pieces(mine, far, dh, dl, inv)
        inv = None
        for iteration in range(1, ITERS + 1):
            early = ahead(pieces[:2], (0, 1), dh, dl, inv=inv)
            if iteration == ITERS:
                break
            other, packed = ahead(pieces[2:], (2, 3), dh, dl, "other", inv, early)

            def own(pieces=pieces, inv=inv, early=early):
                return ahead(pieces[2:], (2, 3), dh, dl, "own", inv, early, None, False)[0]

            mine, far, packed = sum_chips(other, own, packed)
            last_inv = inverse_factor(packed, k)
            pieces = return_pieces(mine, far, dh, dl, inv)
            inv = last_inv
        returned = join(inv, pieces)
        table = gather_rows(returned, bases, pattern_rows)
        images, packed = ahead(pieces[2:], (2, 3), dh, dl, None, inv, early, groups)
    else:
        odds = [masks[b : b + 1, :1] != 0 for b in range(8)]
        images, _ = sum_mode(images, odds)
        returned = sum_pix(backward(inv, images, dh, dl), odds)
        for _ in range(1, ITERS):
            images, packed = forward(returned, dh, dl)
            images, packed = sum_mode(images, odds, packed)
            inv = inverse_factor(packed, k)
            partial = backward(None, images, dh, dl)
            returned = normalise(inv, sum_pix(partial, odds))
        table = gather_rows(returned, bases, pattern_rows)
        images, packed = forward(returned, dh, dl, groups)
    fields, packed = scatter_mode(images, packed)
    inv = inverse_factor(packed, k)
    fields = normalise(inv, fields)
    power = jnp.sum(fields * fields, axis=1)
    power = jnp.broadcast_to((power[:k] + power[k:])[None, :], (8, k))
    power = double_sum(double_sum(power, "mode"), "pix")
    strengths = power[0] / pixels
    channels = end_vectors(inv, table, vectors)
    return (channels.reshape(2, k, modes_total), fields.reshape(2, k, -1), strengths)


def solution(mesh):
    in_specs = (P(None, "pix", "mode"), P(), P(), P())
    out_specs = (P(), P(None, None, ("pix", "mode")), P())
    return jax.shard_map(
        measure, mesh=mesh, in_specs=in_specs, out_specs=out_specs, check_vma=False
    )
```
